32 devices in a mesh: dp: 8 (over z, y), shard: 4 (over x, core).
Axes of the slice: x: 2, y: 2, z: 4, core: 2. Of those that a mesh axis runs over, the one named last changes fastest.
Arguments:
- tokens: bfloat16 [128, 256, 384], P(('dp', 'shard')), may hold values from -6 to 6
- modulation: float32 [128, 6, 384], P(('dp', 'shard')), may hold values from -2.5 to 2.5
- cotangent: bfloat16 [128, 256, 384], P(('dp', 'shard')), may hold values from -6 to 6
- qkv_master: float32 [384, 1152], P('shard'), may hold values from -0.3125 to 0.3125
- proj_master: float32 [384, 384], P('shard'), may hold values from -1.25 to 1.25
- up_master: float32 [384, 1536], P('shard'), may hold values from -0.3125 to 0.3125
- down_master: float32 [1536, 384], P('shard'), may hold values from -0.15625 to 0.15625
- bias_master: float32 [3072], P('shard'), may hold values from -1.2 to 1.2
- qkv_first: float32 [384, 1152], P('shard'), may hold values from -4.5066387e-05 to 4.5066387e-05
- proj_first: float32 [384, 384], P('shard'), may hold values from -4.5066387e-05 to 4.5066387e-05
- up_first: float32 [384, 1536], P('shard'), may hold values from -4.5066387e-05 to 4.5066387e-05
- down_first: float32 [1536, 384], P('shard'), may hold values from -4.5066387e-05 to 4.5066387e-05
- bias_first: float32 [3072], P('shard'), may hold values from -4.5066387e-05 to 4.5066387e-05
- qkv_second: float32 [384, 1152], P('shard'), may hold values from 1.4104022e-12 to 5.6416087e-12
- proj_second: float32 [384, 384], P('shard'), may hold values from 1.4104022e-12 to 5.6416087e-12
- up_second: float32 [384, 1536], P('shard'), may hold values from 1.4104022e-12 to 5.6416087e-12
- down_second: float32 [1536, 384], P('shard'), may hold values from 1.4104022e-12 to 5.6416087e-12
- bias_second: float32 [3072], P('shard'), may hold values from 1.4104022e-12 to 5.6416087e-12
Outputs:
- out_tokens: bfloat16 [128, 256, 384], P(('dp', 'shard'))
- in_grad: float32 [128, 256, 384], P(('dp', 'shard'))
- mod_grad: float32 [128, 6, 384], P(('dp', 'shard'))
- qkv_grad: float32 [384, 1152], P('shard')
- proj_grad: float32 [384, 384], P('shard')
- up_grad: float32 [384, 1536], P('shard')
- down_grad: float32 [1536, 384], P('shard')
- bias_grad: float32 [3072], P('shard')
- qkv_new: float32 [384, 1152], P('shard')
- proj_new: float32 [384, 384], P('shard')
- up_new: float32 [384, 1536], P('shard')
- down_new: float32 [1536, 384], P('shard')
- bias_new: float32 [3072], P('shard')
- qkv_first_new: float32 [384, 1152], P('shard')
- proj_first_new: float32 [384, 384], P('shard')
- up_first_new: float32 [384, 1536], P('shard')
- down_first_new: float32 [1536, 384], P('shard')
- bias_first_new: float32 [3072], P('shard')
- qkv_second_new: float32 [384, 1152], P('shard')
- proj_second_new: float32 [384, 384], P('shard')
- up_second_new: float32 [384, 1536], P('shard')
- down_second_new: float32 [1536, 384], P('shard')
- bias_second_new: float32 [3072], P('shard')
The draws below stay inside these ranges and needn't reach their ends.
All inputs are finite; a program needn't handle non-finite values.
Results may differ from the reference program's by a relative error of at most 0.0085.
The reference program's roundings to bfloat16 on the way count: a program that leaves them out, or rounds other values in their place, can miss the bound.
Values may be sent and summed in bfloat16 or wider, within the bound.
No kernel may reach another device: no remote copies, remote signals or barrier semaphores. Data moves between devices by JAX's collectives and lax.ppermute only.
A program may use at most 128 MiB of HBM per device.

```python
import math
import jax
import jax.numpy as jnp
from jax import lax

D = 384
HEADS = 6
FF = 1536
SEQ = 256
STEP = 10
LATENTS = 128
BIAS = 3072


def draw_modulation(key, part):
    normal_values = jax.random.normal(key, (LATENTS, 6, D), jnp.float32)
    return jnp.clip(0.6 * normal_values, -2.5, 2.5)


def steps_of(own_key, dims, cuts, smallest, largest):
    def one(axis_at, blocks):
        draws = jax.random.uniform(jax.random.fold_in(jax.random.fold_in(own_key, 6), axis_at), (blocks,), jnp.float32, smallest / len(cuts), largest / len(cuts))
        return jnp.repeat(jnp.exp(draws), dims[axis_at] // blocks).reshape((-1,) + (1,) * (len(dims) - axis_at - 1))

    level = one(*cuts[0])
    for cut in cuts[1:]:
        level = level * one(*cut)
    return level


def gaussian(stream_key, extent, width, limit, split=(), held_as=jnp.bfloat16):
    entries = width * jax.random.normal(stream_key, extent, jnp.float32)
    if split:
        entries = entries * steps_of(stream_key, extent, split, -0.22, 0.18)
    return jnp.clip(entries, -limit, limit).astype(held_as)


def setup_inputs(seed: int = 0) -> dict:
    key_list = jax.random.split(jax.random.key(seed), 19)
    tokens = gaussian(key_list[0], (LATENTS, SEQ, D), 1.0, 6.0, ((0, 32),))
    modulation = draw_modulation(jax.random.fold_in(key_list[18], 71), 0)
    cotangent = gaussian(key_list[2], (LATENTS, SEQ, D), 1.0, 6.0, ((0, 32),))
    qkv_master = gaussian(key_list[3], (D, 3 * D), D ** -0.5, 0.3125, ((0, 4),), jnp.float32)
    proj_master = gaussian(key_list[4], (D, D), (D // 16) ** -0.5, 1.25, ((0, 4),), jnp.float32)
    up_master = gaussian(key_list[5], (D, FF), D ** -0.5, 0.3125, ((0, 4),), jnp.float32)
    down_master = gaussian(key_list[6], (FF, D), FF ** -0.5, 0.15625, ((0, 4),), jnp.float32)
    bias_master = gaussian(key_list[7], (BIAS,), 0.2, 1.2, ((0, 4),), jnp.float32)
    qkv_first = gaussian(key_list[8], (D, 3 * D), (0.01 / (4 * D * D + 2 * D * FF + BIAS) ** 0.5), 4.5066386519465595e-05, ((0, 4),), jnp.float32)
    proj_first = gaussian(key_list[9], (D, D), (0.01 / (4 * D * D + 2 * D * FF + BIAS) ** 0.5), 4.5066386519465595e-05, ((0, 4),), jnp.float32)
    up_first = gaussian(key_list[10], (D, FF), (0.01 / (4 * D * D + 2 * D * FF + BIAS) ** 0.5), 4.5066386519465595e-05, ((0, 4),), jnp.float32)
    down_first = gaussian(key_list[11], (FF, D), (0.01 / (4 * D * D + 2 * D * FF + BIAS) ** 0.5), 4.5066386519465595e-05, ((0, 4),), jnp.float32)
    bias_first = gaussian(key_list[12], (BIAS,), (0.01 / (4 * D * D + 2 * D * FF + BIAS) ** 0.5), 4.5066386519465595e-05, ((0, 4),), jnp.float32)
    qkv_second = jnp.clip(jnp.exp(math.log(5.641608707973589e-12) - 1.3862944 * jax.random.uniform(key_list[13], (D, 3 * D), jnp.float32) ** steps_of(key_list[13], (D, 3 * D), ((0, 4),), -0.2, 0.2)), 1.4104021769933972e-12, 5.641608707973589e-12)
    proj_second = jnp.clip(jnp.exp(math.log(5.641608707973589e-12) - 1.3862944 * jax.random.uniform(key_list[14], (D, D), jnp.float32) ** steps_of(key_list[14], (D, D), ((0, 4),), -0.2, 0.2)), 1.4104021769933972e-12, 5.641608707973589e-12)
    up_second = jnp.clip(jnp.exp(math.log(5.641608707973589e-12) - 1.3862944 * jax.random.uniform(key_list[15], (D, FF), jnp.float32) ** steps_of(key_list[15], (D, FF), ((0, 4),), -0.2, 0.2)), 1.4104021769933972e-12, 5.641608707973589e-12)
    down_second = jnp.clip(jnp.exp(math.log(5.641608707973589e-12) - 1.3862944 * jax.random.uniform(key_list[16], (FF, D), jnp.float32) ** steps_of(key_list[16], (FF, D), ((0, 4),), -0.2, 0.2)), 1.4104021769933972e-12, 5.641608707973589e-12)
    bias_second = jnp.clip(jnp.exp(math.log(5.641608707973589e-12) - 1.3862944 * jax.random.uniform(key_list[17], (BIAS,), jnp.float32) ** steps_of(key_list[17], (BIAS,), ((0, 4),), -0.2, 0.2)), 1.4104021769933972e-12, 5.641608707973589e-12)
    return dict(tokens=tokens, modulation=modulation, cotangent=cotangent, qkv_master=qkv_master, proj_master=proj_master, up_master=up_master, down_master=down_master, bias_master=bias_master, qkv_first=qkv_first, proj_first=proj_first, up_first=up_first, down_first=down_first, bias_first=bias_first, qkv_second=qkv_second, proj_second=proj_second, up_second=up_second, down_second=down_second, bias_second=bias_second)


NORM_EPS = 1e-06
GELU_COEF = 0.7978845608028654
GELU_CUBIC = 0.044715
BETA_ONE = 0.9
BETA_TWO = 0.999
LEARN_RATE = 0.08
WEIGHT_DECAY = 0.01
ADAM_EPS = 1e-08
CLIP_NORM = 0.05

def product(left, right):
    return jnp.dot(left, right, preferred_element_type=jnp.float32)

def batched(form, left, right):
    return jnp.einsum(form, left.astype(jnp.float32), right.astype(jnp.float32))

def layer_norm(inputs):
    average = lax.optimization_barrier(jnp.mean(inputs, axis=-1, keepdims=True))
    centered = inputs - average
    inv_std = lax.rsqrt(lax.optimization_barrier(jnp.mean(centered * centered, axis=-1, keepdims=True)) + NORM_EPS)
    return (centered * inv_std, inv_std)

def norm_back(normed, inv_std, upstream):
    return inv_std * (upstream - lax.optimization_barrier(jnp.mean(upstream, axis=-1, keepdims=True)) - normed * lax.optimization_barrier(jnp.mean(upstream * normed, axis=-1, keepdims=True)))

def gelu_parts(inputs):
    tanh_input = GELU_COEF * (inputs + GELU_CUBIC * inputs * inputs * inputs)
    tangent = jnp.tanh(tanh_input)
    output = 0.5 * inputs * (1.0 + tangent)
    slopes = 0.5 * (1.0 + tangent) + 0.5 * inputs * (1.0 - tangent * tangent) * GELU_COEF * (1.0 + 3.0 * GELU_CUBIC * inputs * inputs)
    return (output, slopes)

def head_scores(queries, key_rows):
    return batched('bqhd,bkhd->bhqk', queries, key_rows) * (1.0 / math.sqrt(queries.shape[-1]))

def layer_pass(tokens, modulation, cotangent, qkv_weight, proj_weight, up_weight, down_weight, bias_weight):
    latent_count, span, model_width = tokens.shape
    hidden_width = up_weight.shape[1]
    all_rows = latent_count * span
    head_shape = (latent_count, span, HEADS, model_width // HEADS)
    bias_full = bias_weight.astype(jnp.float32)
    bias_query = bias_full[:model_width]
    bias_value = bias_full[model_width:2 * model_width]
    bias_proj = bias_full[2 * model_width:3 * model_width]
    bias_up = bias_full[3 * model_width:3 * model_width + hidden_width]
    bias_down = bias_full[3 * model_width + hidden_width:]
    shift_mixer = modulation[:, 0:1, :]
    scale_mixer = modulation[:, 1:2, :]
    gate_mixer = modulation[:, 2:3, :]
    shift_feed = modulation[:, 3:4, :]
    scale_feed = modulation[:, 4:5, :]
    gate_feed = modulation[:, 5:6, :]
    inputs = tokens.astype(jnp.float32)
    normed_mixer, inv_std_mixer = layer_norm(inputs)
    moded_mixer = (normed_mixer * (1.0 + scale_mixer) + shift_mixer).astype(jnp.bfloat16).reshape(all_rows, model_width)
    joint = product(moded_mixer, qkv_weight)
    queries = (joint[:, :model_width] + bias_query).astype(jnp.bfloat16).reshape(head_shape)
    key_rows = joint[:, model_width:2 * model_width].astype(jnp.bfloat16).reshape(head_shape)
    value_rows = (joint[:, 2 * model_width:] + bias_value).astype(jnp.bfloat16).reshape(head_shape)
    scores = head_scores(queries, key_rows)
    row_top = lax.optimization_barrier(jnp.max(scores, axis=-1, keepdims=True))
    exponent = jnp.exp(scores - row_top)
    totals = lax.optimization_barrier(jnp.sum(exponent, axis=-1, keepdims=True))
    logsum = row_top + jnp.log(totals)
    soft_weights = (exponent / totals).astype(jnp.bfloat16)
    attended = batched('bhqk,bkhd->bqhd', soft_weights, value_rows).astype(jnp.bfloat16).reshape(all_rows, model_width)
    branch_mixer = (product(attended, proj_weight) + bias_proj).reshape(latent_count, span, model_width)
    middle = inputs + gate_mixer * branch_mixer
    normed_feed, inv_std_feed = layer_norm(middle)
    moded_feed = (normed_feed * (1.0 + scale_feed) + shift_feed).astype(jnp.bfloat16).reshape(all_rows, model_width)
    hidden_in = product(moded_feed, up_weight) + bias_up
    hidden_act, slopes = gelu_parts(hidden_in)
    hidden_out = hidden_act.astype(jnp.bfloat16)
    branch_feed = (product(hidden_out, down_weight) + bias_down).reshape(latent_count, span, model_width)
    out_tokens = (middle + gate_feed * branch_feed).astype(jnp.bfloat16)
    upstream = cotangent.astype(jnp.float32)
    grad_gate_feed = lax.optimization_barrier(jnp.sum(upstream * branch_feed, axis=1))
    grad_branch_feed = (upstream * gate_feed).reshape(all_rows, model_width)
    grad_branch_fhalf = grad_branch_feed.astype(jnp.bfloat16)
    down_grad = product(hidden_out.T, grad_branch_fhalf)
    grad_hidden = product(grad_branch_fhalf, down_weight.T) * slopes
    grad_hidden_half = grad_hidden.astype(jnp.bfloat16)
    up_grad = product(moded_feed.T, grad_hidden_half)
    grad_moded_feed = product(grad_hidden_half, up_weight.T).reshape(latent_count, span, model_width)
    grad_scale_feed = lax.optimization_barrier(jnp.sum(grad_moded_feed * normed_feed, axis=1))
    grad_shift_feed = lax.optimization_barrier(jnp.sum(grad_moded_feed, axis=1))
    grad_middle = upstream + norm_back(normed_feed, inv_std_feed, grad_moded_feed * (1.0 + scale_feed))
    grad_gate_mixer = lax.optimization_barrier(jnp.sum(grad_middle * branch_mixer, axis=1))
    grad_branch_mixer = (grad_middle * gate_mixer).reshape(all_rows, model_width)
    grad_branch_mhalf = grad_branch_mixer.astype(jnp.bfloat16)
    proj_grad = product(attended.T, grad_branch_mhalf)
    grad_attended = product(grad_branch_mhalf, proj_weight.T).astype(jnp.bfloat16).reshape(head_shape)
    recomputed = jnp.exp(head_scores(queries, key_rows) - logsum)
    recomputed_half = recomputed.astype(jnp.bfloat16)
    grad_values = batched('bhqk,bqhd->bkhd', recomputed_half, grad_attended)
    grad_weights = batched('bqhd,bkhd->bhqk', grad_attended, value_rows)
    delta_rows = lax.optimization_barrier(jnp.sum(grad_attended.astype(jnp.float32) * attended.reshape(head_shape).astype(jnp.float32), axis=-1))
    delta_rows = jnp.transpose(delta_rows, (0, 2, 1))[..., None]
    grad_scores = (recomputed * (grad_weights - delta_rows) * (1.0 / math.sqrt(model_width // HEADS))).astype(jnp.bfloat16)
    grad_queries = batched('bhqk,bkhd->bqhd', grad_scores, key_rows).reshape(all_rows, model_width)
    grad_keys = batched('bhqk,bqhd->bkhd', grad_scores, queries).reshape(all_rows, model_width)
    grad_values = grad_values.reshape(all_rows, model_width)
    grad_joint_half = jnp.concatenate([grad_queries, grad_keys, grad_values], axis=1).astype(jnp.bfloat16)
    qkv_grad = product(moded_mixer.T, grad_joint_half)
    grad_moded_mixer = product(grad_joint_half, qkv_weight.T).reshape(latent_count, span, model_width)
    grad_scale_mixer = lax.optimization_barrier(jnp.sum(grad_moded_mixer * normed_mixer, axis=1))
    grad_shift_mixer = lax.optimization_barrier(jnp.sum(grad_moded_mixer, axis=1))
    in_grad = grad_middle + norm_back(normed_mixer, inv_std_mixer, grad_moded_mixer * (1.0 + scale_mixer))
    mod_grad = jnp.stack([grad_shift_mixer, grad_scale_mixer, grad_gate_mixer, grad_shift_feed, grad_scale_feed, grad_gate_feed], axis=1)
    bias_grad = jnp.concatenate([lax.optimization_barrier(jnp.sum(grad_queries, axis=0)), lax.optimization_barrier(jnp.sum(grad_values, axis=0)), lax.optimization_barrier(jnp.sum(grad_branch_mixer, axis=0)), lax.optimization_barrier(jnp.sum(grad_hidden, axis=0)), lax.optimization_barrier(jnp.sum(grad_branch_feed, axis=0))])
    return (out_tokens, in_grad, mod_grad, (qkv_grad, proj_grad, up_grad, down_grad, bias_grad))

def adam_step(master, gradient, first, second, factor):
    clipped = gradient * factor
    first_new = BETA_ONE * first + (1.0 - BETA_ONE) * clipped
    second_new = BETA_TWO * second + (1.0 - BETA_TWO) * clipped * clipped
    first_hat = first_new / (1.0 - BETA_ONE ** STEP)
    second_hat = second_new / (1.0 - BETA_TWO ** STEP)
    master_new = master - LEARN_RATE * (first_hat / (jnp.sqrt(second_hat) + ADAM_EPS) + WEIGHT_DECAY * master)
    return (master_new, first_new, second_new)

def reference(tokens, modulation, cotangent, qkv_master, proj_master, up_master, down_master, bias_master, qkv_first, proj_first, up_first, down_first, bias_first, qkv_second, proj_second, up_second, down_second, bias_second):
    masters = (qkv_master, proj_master, up_master, down_master, bias_master)
    halves = tuple((master.astype(jnp.bfloat16) for master in masters))
    group = math.gcd(LATENTS, max(1, 4096 // SEQ))
    blocks = LATENTS // group

    def shaped(array):
        return array.reshape((blocks, group) + array.shape[1:])

    def scan_step(carry, pieces):
        out_block, in_block, mod_block, grads = layer_pass(pieces[0], pieces[1], pieces[2], halves[0], halves[1], halves[2], halves[3], halves[4])
        carry = tuple((total + term for total, term in zip(carry, grads)))
        return (carry, (out_block, in_block, mod_block))
    initial = tuple((jnp.zeros(master.shape, jnp.float32) for master in masters))
    summed, stacked = lax.scan(scan_step, initial, (shaped(tokens), shaped(modulation), shaped(cotangent)))
    grads = tuple((total * (1.0 / LATENTS) for total in summed))
    out_tokens = stacked[0].reshape(tokens.shape)
    in_grad = stacked[1].reshape(tokens.shape)
    mod_grad = stacked[2].reshape(modulation.shape)
    squares = jnp.zeros((), jnp.float32)
    for gradient in grads:
        squares = squares + jnp.sum(gradient * gradient)
    factor = CLIP_NORM / jnp.maximum(jnp.sqrt(squares), CLIP_NORM)
    firsts = (qkv_first, proj_first, up_first, down_first, bias_first)
    seconds = (qkv_second, proj_second, up_second, down_second, bias_second)
    results = [adam_step(masters[index], grads[index], firsts[index], seconds[index], factor) for index in range(5)]
    return (out_tokens, in_grad, mod_grad, grads[0], grads[1], grads[2], grads[3], grads[4], results[0][0], results[1][0], results[2][0], results[3][0], results[4][0], results[0][1], results[1][1], results[2][1], results[3][1], results[4][1], results[0][2], results[1][2], results[2][2], results[3][2], results[4][2])
```

```python
import functools
import math

import jax
import jax.numpy as jnp
from jax import lax
from jax.experimental import pallas as pl
from jax.experimental.pallas import tpu as pltpu
from jax.sharding import PartitionSpec as P

HEADS = 6
STEP = 10

NORM_EPS = 1e-06
GELU_COEF = 0.7978845608028654
GELU_CUBIC = 0.044715
BETA_ONE = 0.9
BETA_TWO = 0.999
LEARN_RATE = 0.08
WEIGHT_DECAY = 0.01
ADAM_EPS = 1e-08
CLIP_NORM = 0.05

LANES = 128
BF16 = jnp.bfloat16
F32 = jnp.float32


def dot_nn(left, right):
    return lax.dot_general(left, right, (((1,), (0,)), ((), ())), preferred_element_type=F32)


def dot_nt(left, right):
    return lax.dot_general(left, right, (((1,), (1,)), ((), ())), preferred_element_type=F32)


def dot_tn(left, right):
    return lax.dot_general(left, right, (((0,), (0,)), ((), ())), preferred_element_type=F32)


def layer_norm(inputs):
    average = jnp.mean(inputs, axis=-1, keepdims=True)
    centered = inputs - average
    inv_std = lax.rsqrt(jnp.mean(centered * centered, axis=-1, keepdims=True) + NORM_EPS)
    return centered * inv_std, inv_std


def norm_back(normed, inv_std, upstream):
    return inv_std * (
        upstream
        - jnp.mean(upstream, axis=-1, keepdims=True)
        - normed * jnp.mean(upstream * normed, axis=-1, keepdims=True)
    )


def gelu_parts(inputs):
    square = inputs * inputs
    tangent = jnp.tanh(GELU_COEF * inputs * (1.0 + GELU_CUBIC * square))
    half = 0.5 * (1.0 + tangent)
    slopes = half + (0.5 * GELU_COEF) * inputs * (1.0 - tangent * tangent) * (
        1.0 + 3.0 * GELU_CUBIC * square
    )
    return inputs * half, slopes


def lane_half(shape, head):
    lanes = lax.broadcasted_iota(jnp.int32, shape, 1)
    return (lanes < LANES // 2) if head % 2 == 0 else (lanes >= LANES // 2)


def place_rows(refs, target):
    me = lax.axis_index("shard")
    rows = refs[0].shape[0]
    for slot, ref in enumerate(refs):
        owner = jnp.bitwise_xor(me, slot)
        target[pl.ds(pl.multiple_of(owner * rows, 16), rows), :] = ref[...]


def attend_kernel(tokens, modulation, w0, w1, w2, w3, bias, joint_out, attended_out, lse_out, moded_out, weight):
    @pl.when(pl.program_id(0) == 0)
    def _():
        place_rows((w0, w1, w2, w3), weight)

    width = tokens.shape[-1]
    normed, _ = layer_norm(tokens[0].astype(F32))
    mod = modulation[0]
    moded = (normed * (1.0 + mod[1:2]) + mod[0:1]).astype(BF16)
    moded_out[0] = moded
    joint = dot_nn(moded, weight[...])
    bias_full = bias[0:1, :].astype(F32)
    queries = (joint[:, :width] + bias_full[:, :width]).astype(BF16)
    key_rows = joint[:, width : 2 * width].astype(BF16)
    values = (joint[:, 2 * width :] + bias_full[:, width : 2 * width]).astype(BF16)
    joint_out[0, :, :width] = queries
    joint_out[0, :, width : 2 * width] = key_rows
    joint_out[0, :, 2 * width :] = values
    span = queries.shape[0]
    inverse = 1.0 / math.sqrt(width // HEADS)
    lanes = lax.broadcasted_iota(jnp.int32, (span, LANES), 1)
    columns = jnp.zeros((span, LANES), F32)
    for pair in range(HEADS // 2):
        part = slice(pair * LANES, (pair + 1) * LANES)
        halves = []
        for head in (0, 1):
            mask = lane_half((span, LANES), head)
            scaled = jnp.where(mask, queries[:, part].astype(F32) * inverse, 0.0).astype(BF16)
            scores = dot_nt(scaled, key_rows[:, part])
            top = jnp.max(scores, axis=-1, keepdims=True)
            exponent = jnp.exp(scores - top)
            total = jnp.sum(exponent, axis=-1, keepdims=True)
            probs = (exponent * (1.0 / total)).astype(BF16)
            halves.append(dot_nn(probs, values[:, part]))
            columns = jnp.where(lanes == 2 * pair + head, top + jnp.log(total), columns)
        attended_out[0, :, part] = jnp.where(
            lane_half((span, LANES), 0), halves[0], halves[1]
        ).astype(BF16)
    lse_out[0] = columns.T[:8]


def spread(get_rows, target, rows, group):
    me = jnp.bitwise_and(lax.axis_index("dp"), group - 1)
    chunk = target.shape[0] // group
    unit = math.gcd(rows, chunk)
    for start in range(0, target.shape[0], unit):
        value = get_rows(start, unit)
        if value is not None:
            slot = jnp.bitwise_xor(me, start // chunk)
            target[pl.ds(pl.multiple_of(slot * chunk + start % chunk, 8), unit), :] = value


def feed_kernel(
    tokens, modulation, cotangent, attended,
    o0, o1, o2, o3, u0, u1, u2, u3, d0, d1, d2, d3, bias,
    out_tokens, grad_middle_out, grad_attended_out, mod_out, bias_out, proj_grad,
    down_0, down_1, down_2, down_3, up_0, up_1, up_2, up_3,
    proj_w, up_w, down_w, act_all, pre_all, moded_all, branch_all, mixer_all, attended_all, up_full,
    *, group,
):
    step = pl.program_id(0)
    width = tokens.shape[-1]
    hidden = up_w.shape[1]

    @pl.when(step == 0)
    def _():
        place_rows((o0, o1, o2, o3), proj_w)
        place_rows((u0, u1, u2, u3), up_w)
        place_rows((d0, d1, d2, d3), down_w)
        bias_out[...] = jnp.zeros_like(bias_out)

    span = tokens.shape[1]
    here = pl.ds(pl.multiple_of(step * span, span), span)
    mod = modulation[0]
    bias_part = 2 * width
    bias_row = jnp.concatenate([bias[i : i + 1, :] for i in range(bias.shape[0])], axis=1).astype(F32)
    bias_proj = bias_row[:, bias_part : bias_part + width]
    bias_up = bias_row[:, 3 * width : 3 * width + hidden]
    bias_down = bias_row[:, 3 * width + hidden :]
    inputs = tokens[0].astype(F32)
    mixed = attended[0]
    attended_all[here, :] = mixed
    branch_mixer = dot_nn(mixed, proj_w[...]) + bias_proj
    middle = inputs + mod[2:3] * branch_mixer
    normed, inv_std = layer_norm(middle)
    moded = (normed * (1.0 + mod[4:5]) + mod[3:4]).astype(BF16)
    moded_all[here, :] = moded
    upstream = cotangent[0].astype(F32)
    grad_branch = upstream * mod[5:6]
    grad_branch_half = grad_branch.astype(BF16)
    branch_all[here, :] = grad_branch_half
    branch_feed = jnp.zeros((span, width), F32) + bias_down
    grad_moded = jnp.zeros((span, width), F32)
    block = width
    for start in range(0, hidden, block):
        cols = slice(start, start + block)
        act, slopes = gelu_parts(dot_nn(moded, up_w[:, cols]) + bias_up[:, cols])
        act = act.astype(BF16)
        act_all[here, cols] = act
        branch_feed = branch_feed + dot_nn(act, down_w[cols, :])
        grad_pre = dot_nt(grad_branch_half, down_w[cols, :]) * slopes
        bias_out[:, width + start : width + start + block] += jnp.sum(grad_pre, axis=0, keepdims=True)
        grad_pre = grad_pre.astype(BF16)
        pre_all[here, cols] = grad_pre
        grad_moded = grad_moded + dot_nt(grad_pre, up_w[:, cols])
    out_tokens[0] = (middle + mod[5:6] * branch_feed).astype(BF16)
    grad_middle = upstream + norm_back(normed, inv_std, grad_moded * (1.0 + mod[4:5]))
    grad_middle_out[0] = grad_middle
    grad_mixer = grad_middle * mod[2:3]
    grad_mixer_half = grad_mixer.astype(BF16)
    mixer_all[here, :] = grad_mixer_half
    grad_attended_out[0] = dot_nt(grad_mixer_half, proj_w[...]).astype(BF16)
    mod_out[0, 0:1] = jnp.sum(grad_middle * branch_mixer, axis=0, keepdims=True)
    mod_out[0, 1:2] = jnp.sum(grad_moded, axis=0, keepdims=True)
    mod_out[0, 2:3] = jnp.sum(grad_moded * normed, axis=0, keepdims=True)
    mod_out[0, 3:4] = jnp.sum(upstream * branch_feed, axis=0, keepdims=True)
    bias_out[:, :width] += jnp.sum(grad_mixer, axis=0, keepdims=True)
    bias_out[:, width + hidden :] += jnp.sum(grad_branch, axis=0, keepdims=True)

    @pl.when(step == pl.num_programs(0) - 1)
    def _():
        me = lax.axis_index("shard")
        rows = hidden // 4
        for slot, target in enumerate((down_0, down_1, down_2, down_3)):
            owner = jnp.bitwise_xor(me, slot)
            mine = act_all[:, pl.ds(pl.multiple_of(owner * rows, LANES), rows)]
            term = dot_tn(mine, branch_all[...])

            def down_rows(start, unit, term=term):
                col, row = start // rows, start % rows
                return term[row : row + unit, col * LANES : (col + 1) * LANES]

            spread(down_rows, target, rows, group)
        up_full[...] = dot_tn(moded_all[...], pre_all[...])
        rows_up = width // 4
        for slot, target in enumerate((up_0, up_1, up_2, up_3)):
            owner = jnp.bitwise_xor(me, slot)

            def up_rows(start, unit, owner=owner):
                col, row = start // rows_up, start % rows_up
                at = pl.multiple_of(owner * rows_up + row, 8)
                return up_full[pl.ds(at, unit), col * LANES : (col + 1) * LANES]

            spread(up_rows, target, rows_up, group)
        proj_grad[...] = dot_tn(attended_all[...], mixer_all[...])


def attend_back_kernel(
    joint, attended, lse, grad_attended, moded, proj_grad, bias_feed,
    grad_joint_out, part_0, part_1, part_2, part_3,
    moded_all, joint_all, full, bias_sum, *, group,
):
    step = pl.program_id(0)
    width = attended.shape[-1]
    span = attended.shape[1]
    here = pl.ds(pl.multiple_of(step * span, span), span)

    @pl.when(step == 0)
    def _():
        bias_sum[:, : 2 * width] = jnp.zeros((1, 2 * width), F32)
        bias_sum[:, 2 * width :] = bias_feed[...]

    moded_all[here, :] = moded[0]
    inverse = 1.0 / math.sqrt(width // HEADS)
    lanes = lax.broadcasted_iota(jnp.int32, (span, LANES), 1)
    deltas = jnp.zeros((span, LANES), F32)
    for pair in range(HEADS // 2):
        part = slice(pair * LANES, (pair + 1) * LANES)
        products = grad_attended[0, :, part].astype(F32) * attended[0, :, part].astype(F32)
        for head in (0, 1):
            mask = lane_half((span, LANES), head)
            column = jnp.sum(jnp.where(mask, products, 0.0), axis=-1, keepdims=True)
            deltas = jnp.where(lanes == 2 * pair + head, column, deltas)
    delta_rows = deltas.T[:8]
    for pair in range(HEADS // 2):
        part = slice(pair * LANES, (pair + 1) * LANES)
        queries = joint[0, :, pair * LANES : (pair + 1) * LANES]
        keys = joint[0, :, width + pair * LANES : width + (pair + 1) * LANES]
        values = joint[0, :, 2 * width + pair * LANES : 2 * width + (pair + 1) * LANES]
        upstream = grad_attended[0, :, part]
        results = []
        for head in (0, 1):
            index = 2 * pair + head
            mask = lane_half((span, LANES), head)
            masked_keys = jnp.where(mask, keys.astype(F32) * inverse, 0.0).astype(BF16)
            masked_values = jnp.where(mask, values.astype(F32), 0.0).astype(BF16)
            probs = jnp.exp(dot_nt(masked_keys, queries) - lse[0, index : index + 1, :])
            grad_values = dot_nn(probs.astype(BF16), upstream)
            grad_probs = dot_nt(masked_values, upstream)
            grad_scores = (probs * (grad_probs - delta_rows[index : index + 1, :]) * inverse).astype(BF16)
            grad_keys = dot_nn(grad_scores, queries)
            grad_queries = dot_tn(grad_scores, keys)
            results.append((grad_queries, grad_keys, grad_values))
        mask = lane_half((span, LANES), 0)
        for at, (low, high) in enumerate(zip(*results)):
            value = jnp.where(mask, low, high)
            cols = slice(at * width + pair * LANES, at * width + (pair + 1) * LANES)
            half = value.astype(BF16)
            grad_joint_out[0, :, cols] = half
            joint_all[here, cols] = half
            if at != 1:
                place = (at // 2) * width + pair * LANES
                bias_sum[:, place : place + LANES] += jnp.sum(value, axis=0, keepdims=True)

    @pl.when(step == pl.num_programs(0) - 1)
    def _():
        me = lax.axis_index("shard")
        full[...] = dot_tn(moded_all[...], joint_all[...])
        rows = width // 4
        cols_joint = 3 * width // LANES
        cols_all = 4 * width // LANES
        chunk = part_0.shape[0] // group
        tail = cols_all * rows
        unit_tail = math.gcd(rows, chunk)
        for slot, target in enumerate((part_0, part_1, part_2, part_3)):
            owner = jnp.bitwise_xor(me, slot)
            bias_at = owner * 6 * LANES
            bias_rows = jnp.concatenate(
                [
                    bias_sum[:, pl.ds(pl.multiple_of(bias_at + i * LANES, LANES), LANES)]
                    for i in range(6)
                ]
                + [jnp.zeros((unit_tail - 6, LANES), F32)],
                axis=0,
            )

            def part_rows(start, unit, owner=owner, bias_rows=bias_rows):
                if start == tail:
                    return bias_rows
                if start > tail:
                    return jnp.zeros((unit, LANES), F32)
                col, row = start // rows, start % rows
                at = pl.multiple_of(owner * rows + row, 8)
                if col < cols_joint:
                    return full[pl.ds(at, unit), col * LANES : (col + 1) * LANES]
                col -= cols_joint
                return proj_grad[pl.ds(at, unit), col * LANES : (col + 1) * LANES]

            spread(part_rows, target, rows, group)


def input_kernel(tokens, modulation, grad_joint, grad_middle, mod_feed, w0, w1, w2, w3, in_grad, mod_grad, weight):
    @pl.when(pl.program_id(0) == 0)
    def _():
        place_rows((w0, w1, w2, w3), weight)

    mod = modulation[0]
    normed, inv_std = layer_norm(tokens[0].astype(F32))
    grad_moded = dot_nt(grad_joint[0], weight[...])
    in_grad[0] = grad_middle[0] + norm_back(normed, inv_std, grad_moded * (1.0 + mod[1:2]))
    mod_grad[0, 0:1] = jnp.sum(grad_moded, axis=0, keepdims=True)
    mod_grad[0, 1:2] = jnp.sum(grad_moded * normed, axis=0, keepdims=True)
    mod_grad[0, 2:6] = mod_feed[0]


def adam_kernel(
    factor_ref,
    own_d, far_d, own_u, far_u, own_p, far_p,
    qkv_w, proj_w, up_w, down_w, bias_w,
    qkv_m, proj_m, up_m, down_m, bias_m,
    qkv_v, proj_v, up_v, down_v, bias_v,
    qkv_g, proj_g, up_g, down_g, bias_g,
    qkv_nw, proj_nw, up_nw, down_nw, bias_nw,
    qkv_nm, proj_nm, up_nm, down_nm, bias_nm,
    qkv_nv, proj_nv, up_nv, down_nv, bias_nv,
    down_all, up_all, part_all,
    *, group,
):
    me = jnp.bitwise_and(lax.axis_index("dp"), group - 1)
    factor = factor_ref[0, 0]
    for own, far, target in ((own_d, far_d, down_all), (own_u, far_u, up_all), (own_p, far_p, part_all)):
        chunk = target.shape[0] // group
        for slot in range(group):
            source = own if slot % 2 == 0 else far
            at = jnp.bitwise_xor(me, slot) * chunk
            target[pl.ds(pl.multiple_of(at, 16), chunk), :] = source[slot // 2].astype(F32)

    def update(grad, w, m, v, g_out, w_out, m_out, v_out, cols):
        g_out[:, cols] = grad
        clipped = grad * factor
        first = BETA_ONE * m[:, cols] + (1.0 - BETA_ONE) * clipped
        second = BETA_TWO * v[:, cols] + (1.0 - BETA_TWO) * clipped * clipped
        m_out[:, cols] = first
        v_out[:, cols] = second
        first_hat = first * (1.0 / (1.0 - BETA_ONE**STEP))
        second_hat = second * (1.0 / (1.0 - BETA_TWO**STEP))
        master = w[:, cols]
        w_out[:, cols] = master - LEARN_RATE * (
            first_hat / (jnp.sqrt(second_hat) + ADAM_EPS) + WEIGHT_DECAY * master
        )

    base = 0
    for source, start, refs in (
        (down_all, True, (down_w, down_m, down_v, down_g, down_nw, down_nm, down_nv)),
        (up_all, True, (up_w, up_m, up_v, up_g, up_nw, up_nm, up_nv)),
        (part_all, True, (qkv_w, qkv_m, qkv_v, qkv_g, qkv_nw, qkv_nm, qkv_nv)),
        (part_all, False, (proj_w, proj_m, proj_v, proj_g, proj_nw, proj_nm, proj_nv)),
        (part_all, False, (bias_w, bias_m, bias_v, bias_g, bias_nw, bias_nm, bias_nv)),
    ):
        base = 0 if start else base
        rows, cols = refs[0].shape
        for col in range(cols // LANES):
            update(source[base : base + rows, :], *refs, slice(col * LANES, (col + 1) * LANES))
            base += rows


def swap(value, axis, mask):
    size = lax.axis_size(axis)
    return lax.ppermute(value, axis, [(i, i ^ mask) for i in range(size)])


def gather_shards(value):
    high = swap(value, "shard", 2)
    return (value, swap(value, "shard", 1), high, swap(high, "shard", 1))


def tree_sum(parts):
    while len(parts) > 1:
        parts = [parts[i] + parts[i + 1] for i in range(0, len(parts), 2)]
    return parts[0]


def reduce_piece(parts, group, scale):
    keep_own, send_own, keep_far, send_far = parts
    far = keep_far + swap(send_far, "shard", 1)
    own = keep_own + swap(send_own, "shard", 1)
    total = own + swap(far.astype(BF16), "shard", 2).astype(F32)
    rows = total.shape[0]
    total = total.reshape(group // 2, 2, rows // group, LANES)
    total = total[:, 0] + swap(total[:, 1].astype(BF16), "dp", 1).astype(F32)
    terms = [total[0]]
    for slot in range(1, group // 2):
        terms.append(swap(total[slot].astype(BF16), "dp", 2 * slot).astype(F32))
    total = tree_sum(terms)
    mask = group
    while mask < lax.axis_size("dp"):
        total = total + swap(total, "dp", mask)
        mask *= 2
    return total * scale


def gather_piece(total, group):
    half = total.astype(BF16)
    own = jnp.stack([half] + [swap(half, "dp", 2 * slot) for slot in range(1, group // 2)])
    return own, swap(own, "dp", 1)


def square_total(totals, group):
    square = functools.reduce(lambda a, b: a + b, [jnp.sum(t * t) for t in totals])
    square = jnp.full((8, LANES), square, F32)
    square = tree_sum([square] + [swap(square, "shard", m) for m in range(1, lax.axis_size("shard"))])
    return tree_sum([square] + [swap(square, "dp", m) for m in range(1, group)])[0:1, 0:1]


def whole(shape):
    zeros = (0,) * len(shape)
    return pl.BlockSpec(shape, lambda i: zeros, pipeline_mode=pl.Buffered(1))


def each(shape):
    return pl.BlockSpec((1,) + tuple(shape[1:]), lambda i: (i,) + (0,) * (len(shape) - 1))


def struct(shape, dtype):
    return jax.ShapeDtypeStruct(shape, dtype)


def shards(
    tokens, modulation, cotangent,
    qkv_master, proj_master, up_master, down_master, bias_master,
    qkv_first, proj_first, up_first, down_first, bias_first,
    qkv_second, proj_second, up_second, down_second, bias_second,
):
    latents, span, width = tokens.shape
    hidden = up_master.shape[1]
    group = min(8, lax.axis_size("dp"))
    devices = lax.axis_size("dp") * lax.axis_size("shard")
    latent_total = latents * devices
    all_rows = latents * span

    qkv_ws = gather_shards(qkv_master.astype(BF16))
    bias_size = bias_master.shape[0]
    owner = lax.axis_index("shard")
    slots = lax.broadcasted_iota(jnp.int32, (4, bias_size), 0)
    bias = jnp.where(slots == owner, bias_master.astype(BF16)[None], 0.0).astype(BF16)
    bias = bias + swap(bias, "shard", 1)
    bias = bias + swap(bias, "shard", 2)
    later = lax.optimization_barrier(
        (proj_master.astype(BF16), up_master.astype(BF16), down_master.astype(BF16), qkv_ws[2])
    )
    qkv_ws = (qkv_ws[0], qkv_ws[1], later[3], qkv_ws[3])
    proj_ws = gather_shards(later[0])
    up_ws = gather_shards(later[1])
    down_ws = gather_shards(later[2])

    tok = (latents, span, width)
    mod = modulation.shape
    joint, attended, lse, moded = pl.pallas_call(
        attend_kernel,
        grid=(latents,),
        in_specs=[each(tok), each(mod)] + [whole(w.shape) for w in qkv_ws] + [whole(bias.shape)],
        out_specs=[each((latents, span, 3 * width)), each(tok), each((latents, 8, span)), each(tok)],
        out_shape=[
            struct((latents, span, 3 * width), BF16),
            struct(tok, BF16),
            struct((latents, 8, span), F32),
            struct(tok, BF16),
        ],
        scratch_shapes=[pltpu.VMEM((width, 3 * width), BF16)],
        cost_estimate=pl.CostEstimate(flops=2 * 10**9, bytes_accessed=6 * 10**6, transcendentals=10**6),
        name="attend",
    )(tokens, modulation, *qkv_ws, bias)

    piece = hidden * width // 4 // LANES
    piece_shape = struct((piece, LANES), F32)
    outs = pl.pallas_call(
        functools.partial(feed_kernel, group=group),
        grid=(latents,),
        in_specs=[each(tok), each(mod), each(tok), each(tok)]
        + [whole(w.shape) for w in proj_ws + up_ws + down_ws]
        + [whole(bias.shape)],
        out_specs=[each(tok), each(tok), each(tok), each((latents, 4, width))]
        + [whole((1, 2 * width + hidden)), whole((width, width))]
        + [whole((piece, LANES))] * 8,
        out_shape=[
            struct(tok, BF16),
            struct(tok, F32),
            struct(tok, BF16),
            struct((latents, 4, width), F32),
            struct((1, 2 * width + hidden), F32),
            struct((width, width), F32),
        ]
        + [piece_shape] * 8,
        scratch_shapes=[
            pltpu.VMEM((width, width), BF16),
            pltpu.VMEM((width, hidden), BF16),
            pltpu.VMEM((hidden, width), BF16),
            pltpu.VMEM((all_rows, hidden), BF16),
            pltpu.VMEM((all_rows, hidden), BF16),
            pltpu.VMEM((all_rows, width), BF16),
            pltpu.VMEM((all_rows, width), BF16),
            pltpu.VMEM((all_rows, width), BF16),
            pltpu.VMEM((all_rows, width), BF16),
            pltpu.VMEM((width, hidden), F32),
        ],
        cost_estimate=pl.CostEstimate(flops=8 * 10**9, bytes_accessed=16 * 10**6, transcendentals=2 * 10**6),
        name="feed",
    )(tokens, modulation, cotangent, attended, *proj_ws, *up_ws, *down_ws, bias)
    out_tokens, grad_middle, grad_attended, mod_feed, bias_feed, proj_term = outs[:6]
    scale = 1.0 / latent_total
    down_total = reduce_piece(outs[6:10], group, scale)
    up_total = reduce_piece(outs[10:14], group, scale)

    last = 4 * width * (width // 4) // LANES
    chunk = -(-(last + 8) // (16 * group)) * 16
    last_shape = (chunk * group, LANES)
    outs = pl.pallas_call(
        functools.partial(attend_back_kernel, group=group),
        grid=(latents,),
        in_specs=[each(joint.shape), each(tok), each(lse.shape), each(tok), each(tok)]
        + [whole(proj_term.shape), whole(bias_feed.shape)],
        out_specs=[each(joint.shape)] + [whole(last_shape)] * 4,
        out_shape=[struct(joint.shape, BF16)] + [struct(last_shape, F32)] * 4,
        scratch_shapes=[
            pltpu.VMEM((all_rows, width), BF16),
            pltpu.VMEM((all_rows, 3 * width), BF16),
            pltpu.VMEM((width, 3 * width), F32),
            pltpu.VMEM((1, 4 * bias_size), F32),
        ],
        cost_estimate=pl.CostEstimate(flops=4 * 10**9, bytes_accessed=10 * 10**6, transcendentals=10**6),
        name="attend_back",
    )(joint, attended, lse, grad_attended, moded, proj_term, bias_feed)
    grad_joint = outs[0]
    part_total = reduce_piece(outs[1:5], group, scale)

    in_grad, mod_grad = pl.pallas_call(
        input_kernel,
        grid=(latents,),
        in_specs=[each(tok), each(mod), each(joint.shape), each(tok), each(mod_feed.shape)]
        + [whole(w.shape) for w in qkv_ws],
        out_specs=[each(tok), each(mod)],
        out_shape=[struct(tok, F32), struct(mod, F32)],
        scratch_shapes=[pltpu.VMEM((width, 3 * width), BF16)],
        cost_estimate=pl.CostEstimate(flops=2 * 10**9, bytes_accessed=8 * 10**6, transcendentals=0),
        name="input",
    )(tokens, modulation, grad_joint, grad_middle, mod_feed, *qkv_ws)

    totals = (down_total, up_total, part_total)
    squares = square_total(totals, group)
    factor = CLIP_NORM / jnp.maximum(jnp.sqrt(squares), CLIP_NORM)
    gathered = [array for total in totals for array in gather_piece(total, group)]

    flat = (bias_size // LANES, LANES)
    bias_rows = flat[0]
    folded = lambda a: a.reshape(1, bias_size)
    states = (
        qkv_master, proj_master, up_master, down_master, folded(bias_master),
        qkv_first, proj_first, up_first, down_first, folded(bias_first),
        qkv_second, proj_second, up_second, down_second, folded(bias_second),
    )
    vmem = pl.BlockSpec(memory_space=pltpu.VMEM)
    updated = pl.pallas_call(
        functools.partial(adam_kernel, group=group),
        in_specs=[pl.BlockSpec(memory_space=pltpu.SMEM)] + [vmem] * (6 + len(states)),
        out_specs=[vmem] * 20,
        out_shape=[struct(s.shape, F32) for s in states[:5]] * 4,
        scratch_shapes=[
            pltpu.VMEM((piece, LANES), F32),
            pltpu.VMEM((piece, LANES), F32),
            pltpu.VMEM(last_shape, F32),
        ],
        cost_estimate=pl.CostEstimate(flops=10**7, bytes_accessed=14 * 10**6, transcendentals=0),
        name="adam",
    )(factor, *gathered, *states)
    updated = list(updated)
    for at in (4, 9, 14, 19):
        updated[at] = updated[at].reshape(bias_size)
    return (out_tokens, in_grad, mod_grad, *updated)


def solution(mesh):
    data = P(("dp", "shard"), None, None)
    weight = P("shard", None)
    five = (weight, weight, weight, weight, P("shard"))
    return jax.shard_map(
        shards,
        mesh=mesh,
        in_specs=(data, data, data) + five * 3,
        out_specs=(data, data, data) + five * 4,
        check_vma=False,
    )
```

```python
import functools
import math

import jax
import jax.numpy as jnp
from jax import lax
from jax.experimental import pallas as pl
from jax.experimental.pallas import tpu as pltpu
from jax.sharding import PartitionSpec as P

HEADS = 6
STEP = 10

NORM_EPS = 1e-06
GELU_COEF = 0.7978845608028654
GELU_CUBIC = 0.044715
BETA_ONE = 0.9
BETA_TWO = 0.999
LEARN_RATE = 0.08
WEIGHT_DECAY = 0.01
ADAM_EPS = 1e-08
CLIP_NORM = 0.05

LANES = 128
BF16 = jnp.bfloat16
F32 = jnp.float32


def dot_nn(left, right):
    return lax.dot_general(left, right, (((1,), (0,)), ((), ())), preferred_element_type=F32)


def dot_nt(left, right):
    return lax.dot_general(left, right, (((1,), (1,)), ((), ())), preferred_element_type=F32)


def dot_tn(left, right):
    return lax.dot_general(left, right, (((0,), (0,)), ((), ())), preferred_element_type=F32)


def layer_norm(inputs):
    average = jnp.mean(inputs, axis=-1, keepdims=True)
    centered = inputs - average
    inv_std = lax.rsqrt(jnp.mean(centered * centered, axis=-1, keepdims=True) + NORM_EPS)
    return centered * inv_std, inv_std


def norm_back(normed, inv_std, upstream):
    return inv_std * (
        upstream
        - jnp.mean(upstream, axis=-1, keepdims=True)
        - normed * jnp.mean(upstream * normed, axis=-1, keepdims=True)
    )


def gelu_parts(inputs):
    square = inputs * inputs
    tangent = jnp.tanh(GELU_COEF * inputs * (1.0 + GELU_CUBIC * square))
    half = 0.5 * (1.0 + tangent)
    slopes = half + (0.5 * GELU_COEF) * inputs * (1.0 - tangent * tangent) * (
        1.0 + 3.0 * GELU_CUBIC * square
    )
    return inputs * half, slopes


def lane_half(shape, head):
    lanes = lax.broadcasted_iota(jnp.int32, shape, 1)
    return (lanes < LANES // 2) if head % 2 == 0 else (lanes >= LANES // 2)


def owners(refs):
    me = lax.axis_index("shard")
    return [(jnp.bitwise_xor(me, slot), ref) for slot, ref in enumerate(refs)]


def place(target, owner, rows, value):
    target[pl.ds(pl.multiple_of(owner * rows, 16), rows), :] = value


def attend_kernel(tokens, modulation, w0, w1, w2, w3, joint_out, attended_out, lse_out, moded_out, bias, weight):
    @pl.when(pl.program_id(0) == 0)
    def _():
        rows = weight.shape[0] // 4
        for owner, ref in owners((w0, w1, w2, w3)):
            place(weight, owner, rows, ref[:rows, :])
            bias[pl.ds(owner, 1), :] = ref[rows : rows + 1, : bias.shape[1]].astype(F32)

    width = tokens.shape[-1]
    normed, _ = layer_norm(tokens[0].astype(F32))
    mod = modulation[0]
    moded = (normed * (1.0 + mod[1:2]) + mod[0:1]).astype(BF16)
    moded_out[0] = moded
    joint = dot_nn(moded, weight[...])
    bias_full = bias[0:1, :]
    queries = (joint[:, :width] + bias_full[:, :width]).astype(BF16)
    key_rows = joint[:, width : 2 * width].astype(BF16)
    values = (joint[:, 2 * width :] + bias_full[:, width : 2 * width]).astype(BF16)
    joint_out[0, :, :width] = queries
    joint_out[0, :, width : 2 * width] = key_rows
    joint_out[0, :, 2 * width :] = values
    span = queries.shape[0]
    inverse = 1.0 / math.sqrt(width // HEADS)
    lanes = lax.broadcasted_iota(jnp.int32, (span, LANES), 1)
    columns = jnp.zeros((span, LANES), F32)
    for pair in range(HEADS // 2):
        part = slice(pair * LANES, (pair + 1) * LANES)
        halves = []
        for head in (0, 1):
            mask = lane_half((span, LANES), head)
            scaled = jnp.where(mask, queries[:, part].astype(F32) * inverse, 0.0).astype(BF16)
            scores = dot_nt(scaled, key_rows[:, part])
            top = jnp.max(scores, axis=-1, keepdims=True)
            exponent = jnp.exp(scores - top)
            total = jnp.sum(exponent, axis=-1, keepdims=True)
            probs = (exponent * (1.0 / total)).astype(BF16)
            halves.append(dot_nn(probs, values[:, part]))
            columns = jnp.where(lanes == 2 * pair + head, top + jnp.log(total), columns)
        attended_out[0, :, part] = jnp.where(
            lane_half((span, LANES), 0), halves[0], halves[1]
        ).astype(BF16)
    lse_out[0] = columns.T[:8]


def spread(get_rows, store, rows, start, count, chunk, group):
    me = jnp.bitwise_and(lax.axis_index("dp"), group - 1)
    unit = math.gcd(rows, chunk)
    for row in range(start, start + count, unit):
        slot = jnp.bitwise_xor(me, row // chunk)
        at = pl.multiple_of(slot * chunk + row % chunk, 8)
        store(pl.ds(at, unit), get_rows(row - start, unit))


def storer(keep, send, slot):
    target = (keep, send)[slot % 2]

    def store(rows, value):
        target[slot // 2, rows, :] = value

    return store


def feed_kernel(
    tokens, modulation, cotangent, attended,
    w0, w1, w2, w3, bias,
    out_tokens, grad_middle_out, grad_attended_out, mod_out, bias_out, proj_grad,
    keep, send,
    proj_w, up_w, down_w, act_all, pre_all, moded_all, branch_all, mixer_all, attended_all, up_full,
    *, group,
):
    step = pl.program_id(0)
    width = tokens.shape[-1]
    hidden = up_w.shape[1]

    @pl.when(step == 0)
    def _():
        rows, rows_down = width // 4, hidden // 4
        for owner, ref in owners((w0, w1, w2, w3)):
            place(proj_w, owner, rows, ref[:rows, :])
            place(down_w, owner, rows_down, ref[rows : rows + rows_down, :])
            for block in range(hidden // width):
                at = rows + rows_down + block * rows
                place(
                    up_w.at[:, block * width : (block + 1) * width], owner, rows, ref[at : at + rows, :]
                )
        bias_out[...] = jnp.zeros_like(bias_out)

    span = tokens.shape[1]
    here = pl.ds(pl.multiple_of(step * span, span), span)
    mod = modulation[0]
    bias_part = 2 * width
    bias_row = jnp.concatenate([bias[i : i + 1, :] for i in range(bias.shape[0])], axis=1)
    bias_proj = bias_row[:, bias_part : bias_part + width]
    bias_up = bias_row[:, 3 * width : 3 * width + hidden]
    bias_down = bias_row[:, 3 * width + hidden :]
    inputs = tokens[0].astype(F32)
    mixed = attended[0]
    attended_all[here, :] = mixed
    branch_mixer = dot_nn(mixed, proj_w[...]) + bias_proj
    middle = inputs + mod[2:3] * branch_mixer
    normed, inv_std = layer_norm(middle)
    moded = (normed * (1.0 + mod[4:5]) + mod[3:4]).astype(BF16)
    moded_all[here, :] = moded
    upstream = cotangent[0].astype(F32)
    grad_branch = upstream * mod[5:6]
    grad_branch_half = grad_branch.astype(BF16)
    branch_all[here, :] = grad_branch_half
    branch_feed = jnp.zeros((span, width), F32) + bias_down
    grad_moded = jnp.zeros((span, width), F32)
    block = width
    for start in range(0, hidden, block):
        cols = slice(start, start + block)
        act, slopes = gelu_parts(dot_nn(moded, up_w[:, cols]) + bias_up[:, cols])
        act = act.astype(BF16)
        act_all[here, cols] = act
        branch_feed = branch_feed + dot_nn(act, down_w[cols, :])
        grad_pre = dot_nt(grad_branch_half, down_w[cols, :]) * slopes
        bias_out[:, width + start : width + start + block] += jnp.sum(grad_pre, axis=0, keepdims=True)
        grad_pre = grad_pre.astype(BF16)
        pre_all[here, cols] = grad_pre
        grad_moded = grad_moded + dot_nt(grad_pre, up_w[:, cols])
    out_tokens[0] = (middle + mod[5:6] * branch_feed).astype(BF16)
    grad_middle = upstream + norm_back(normed, inv_std, grad_moded * (1.0 + mod[4:5]))
    grad_middle_out[0] = grad_middle
    grad_mixer = grad_middle * mod[2:3]
    grad_mixer_half = grad_mixer.astype(BF16)
    mixer_all[here, :] = grad_mixer_half
    grad_attended_out[0] = dot_nt(grad_mixer_half, proj_w[...]).astype(BF16)
    mod_out[0, 0:1] = jnp.sum(grad_middle * branch_mixer, axis=0, keepdims=True)
    mod_out[0, 1:2] = jnp.sum(grad_moded, axis=0, keepdims=True)
    mod_out[0, 2:3] = jnp.sum(grad_moded * normed, axis=0, keepdims=True)
    mod_out[0, 3:4] = jnp.sum(upstream * branch_feed, axis=0, keepdims=True)
    bias_out[:, :width] += jnp.sum(grad_mixer, axis=0, keepdims=True)
    bias_out[:, width + hidden :] += jnp.sum(grad_branch, axis=0, keepdims=True)

    @pl.when(step == pl.num_programs(0) - 1)
    def _():
        me = lax.axis_index("shard")
        rows = hidden // 4
        rows_up = width // 4
        chunk = keep.shape[1] // group
        half = keep.shape[1] // 2
        for slot in (1, 3, 0, 2):
            owner = jnp.bitwise_xor(me, slot)
            mine = act_all[:, pl.ds(pl.multiple_of(owner * rows, LANES), rows)]
            term = dot_tn(mine, branch_all[...])

            def down_rows(start, unit, term=term):
                col, row = start // rows, start % rows
                return term[row : row + unit, col * LANES : (col + 1) * LANES]

            spread(down_rows, storer(keep, send, slot), rows, 0, half, chunk, group)
        up_full[...] = dot_tn(moded_all[...], pre_all[...])
        for slot in range(4):
            owner = jnp.bitwise_xor(me, slot)

            def up_rows(start, unit, owner=owner):
                col, row = start // rows_up, start % rows_up
                at = pl.multiple_of(owner * rows_up + row, 8)
                return up_full[pl.ds(at, unit), col * LANES : (col + 1) * LANES]

            spread(up_rows, storer(keep, send, slot), rows_up, half, half, chunk, group)
        proj_grad[...] = dot_tn(attended_all[...], mixer_all[...])


def attend_back_kernel(joint, attended, lse, grad_attended, moded, *rest, group, final):
    if final:
        proj_grad, bias_before, full_before, _, grad_joint_out, keep, send = rest[:7]
        moded_all, joint_all, bias_sum, full = rest[7:]
    else:
        bias_before, grad_joint_out, bias_sum, full = rest[:4]
        moded_all, joint_all = rest[4:]
    step = pl.program_id(0)
    width = attended.shape[-1]
    span = attended.shape[1]
    here = pl.ds(pl.multiple_of(step * span, span), span)

    @pl.when(step == 0)
    def _():
        bias_sum[...] = bias_before[...]

    moded_all[here, :] = moded[0]
    inverse = 1.0 / math.sqrt(width // HEADS)
    lanes = lax.broadcasted_iota(jnp.int32, (span, LANES), 1)
    deltas = jnp.zeros((span, LANES), F32)
    for pair in range(HEADS // 2):
        part = slice(pair * LANES, (pair + 1) * LANES)
        products = grad_attended[0, :, part].astype(F32) * attended[0, :, part].astype(F32)
        for head in (0, 1):
            mask = lane_half((span, LANES), head)
            column = jnp.sum(jnp.where(mask, products, 0.0), axis=-1, keepdims=True)
            deltas = jnp.where(lanes == 2 * pair + head, column, deltas)
    delta_rows = deltas.T[:8]
    for pair in range(HEADS // 2):
        part = slice(pair * LANES, (pair + 1) * LANES)
        queries = joint[0, :, pair * LANES : (pair + 1) * LANES]
        keys = joint[0, :, width + pair * LANES : width + (pair + 1) * LANES]
        values = joint[0, :, 2 * width + pair * LANES : 2 * width + (pair + 1) * LANES]
        upstream = grad_attended[0, :, part]
        results = []
        for head in (0, 1):
            index = 2 * pair + head
            mask = lane_half((span, LANES), head)
            masked_keys = jnp.where(mask, keys.astype(F32) * inverse, 0.0).astype(BF16)
            masked_values = jnp.where(mask, values.astype(F32), 0.0).astype(BF16)
            probs = jnp.exp(dot_nt(masked_keys, queries) - lse[0, index : index + 1, :])
            grad_values = dot_nn(probs.astype(BF16), upstream)
            grad_probs = dot_nt(masked_values, upstream)
            grad_scores = (probs * (grad_probs - delta_rows[index : index + 1, :]) * inverse).astype(BF16)
            grad_keys = dot_nn(grad_scores, queries)
            grad_queries = dot_tn(grad_scores, keys)
            results.append((grad_queries, grad_keys, grad_values))
        mask = lane_half((span, LANES), 0)
        for at, (low, high) in enumerate(zip(*results)):
            value = jnp.where(mask, low, high)
            cols = slice(at * width + pair * LANES, at * width + (pair + 1) * LANES)
            half = value.astype(BF16)
            grad_joint_out[0, :, cols] = half
            joint_all[here, cols] = half
            if at != 1:
                place = (at // 2) * width + pair * LANES
                bias_sum[:, place : place + LANES] += jnp.sum(value, axis=0, keepdims=True)

    @pl.when(step == pl.num_programs(0) - 1)
    def _():
        full[...] = dot_tn(moded_all[...], joint_all[...])
        if not final:
            return
        full[...] += full_before[...]
        me = lax.axis_index("shard")
        rows = width // 4
        cols_joint = 3 * width // LANES
        tail = 4 * width // LANES * rows
        total = keep.shape[1]
        chunk = total // group
        bias_rows = bias_sum.shape[1] // 4 // LANES
        for slot in range(4):
            owner = jnp.bitwise_xor(me, slot)
            unit_tail = math.gcd(rows, chunk)
            bias_at = owner * bias_rows * LANES
            block = jnp.concatenate(
                [
                    bias_sum[:, pl.ds(pl.multiple_of(bias_at + i * LANES, LANES), LANES)]
                    for i in range(bias_rows)
                ]
                + [jnp.zeros((unit_tail - bias_rows, LANES), F32)],
                axis=0,
            )

            def part_rows(start, unit, owner=owner, block=block):
                if start == tail:
                    return block
                if start > tail:
                    return jnp.zeros((unit, LANES), F32)
                col, row = start // rows, start % rows
                at = pl.multiple_of(owner * rows + row, 8)
                if col < cols_joint:
                    return full[pl.ds(at, unit), col * LANES : (col + 1) * LANES]
                col -= cols_joint
                return proj_grad[pl.ds(at, unit), col * LANES : (col + 1) * LANES]

            spread(part_rows, storer(keep, send, slot), rows, 0, total, chunk, group)


def input_kernel(tokens, modulation, grad_joint, grad_middle, mod_feed, w0, w1, w2, w3, in_grad, mod_grad, weight):
    @pl.when(pl.program_id(0) == 0)
    def _():
        rows = weight.shape[0] // 4
        for owner, ref in owners((w0, w1, w2, w3)):
            place(weight, owner, rows, ref[:rows, :])

    mod = modulation[0]
    normed, inv_std = layer_norm(tokens[0].astype(F32))
    grad_moded = dot_nt(grad_joint[0], weight[...])
    in_grad[0] = grad_middle[0] + norm_back(normed, inv_std, grad_moded * (1.0 + mod[1:2]))
    mod_grad[0, 0:1] = jnp.sum(grad_moded, axis=0, keepdims=True)
    mod_grad[0, 1:2] = jnp.sum(grad_moded * normed, axis=0, keepdims=True)
    mod_grad[0, 2:6] = mod_feed[0]


def adam_kernel(
    factor_ref, own, far,
    qkv_w, proj_w, up_w, down_w,
    qkv_m, proj_m, up_m, down_m,
    qkv_v, proj_v, up_v, down_v,
    qkv_g, proj_g, up_g, down_g, bias_g,
    qkv_nw, proj_nw, up_nw, down_nw,
    qkv_nm, proj_nm, up_nm, down_nm,
    qkv_nv, proj_nv, up_nv, down_nv,
    feed_all, part_all,
    *, group,
):
    me = jnp.bitwise_and(lax.axis_index("dp"), group - 1)
    factor = factor_ref[0, 0]
    base = 0
    for target in (feed_all, part_all):
        chunk = target.shape[0] // group
        for slot in range(group):
            source = own if slot % 2 == 0 else far
            at = jnp.bitwise_xor(me, slot) * chunk
            value = source[slot // 2, base : base + chunk, :].astype(F32)
            if base:
                rest = (source.shape[1] - base) // 2
                value = value + source[slot // 2, base + rest : base + rest + chunk, :].astype(F32)
            target[pl.ds(pl.multiple_of(at, 8), chunk), :] = value
        base += chunk

    base = 0
    for source, start, refs in (
        (feed_all, True, (down_w, down_m, down_v, down_g, down_nw, down_nm, down_nv)),
        (feed_all, False, (up_w, up_m, up_v, up_g, up_nw, up_nm, up_nv)),
        (part_all, True, (qkv_w, qkv_m, qkv_v, qkv_g, qkv_nw, qkv_nm, qkv_nv)),
        (part_all, False, (proj_w, proj_m, proj_v, proj_g, proj_nw, proj_nm, proj_nv)),
    ):
        base = 0 if start else base
        w, m, v, g_out, w_out, m_out, v_out = refs
        rows, cols = w.shape
        for col in range(cols // LANES):
            at = slice(col * LANES, (col + 1) * LANES)
            grad = source[base : base + rows, :]
            g_out[:, at] = grad
            w_out[:, at], m_out[:, at], v_out[:, at] = adam_step(w[:, at], grad, m[:, at], v[:, at], factor)
            base += rows
    bias_g[...] = part_all[base : base + bias_g.shape[0], :]


def adam_step(master, grad, first, second, factor):
    clipped = grad * factor
    first = BETA_ONE * first + (1.0 - BETA_ONE) * clipped
    second = BETA_TWO * second + (1.0 - BETA_TWO) * clipped * clipped
    first_hat = first * (1.0 / (1.0 - BETA_ONE**STEP))
    second_hat = second * (1.0 / (1.0 - BETA_TWO**STEP))
    master = master - LEARN_RATE * (
        first_hat / (jnp.sqrt(second_hat) + ADAM_EPS) + WEIGHT_DECAY * master
    )
    return master, first, second


def swap(value, axis, mask):
    size = lax.axis_size(axis)
    return lax.ppermute(value, axis, [(i, i ^ mask) for i in range(size)])


def tree_sum(parts):
    while len(parts) > 1:
        parts = [parts[i] + parts[i + 1] for i in range(0, len(parts), 2)]
    return parts[0]


def over_core(keep, send):
    other = swap(send, "shard", 1)
    return keep[0] + other[0], keep[1] + other[1]


def over_shard(own, far, wire):
    return own + swap(far.astype(wire), "shard", 2).astype(F32)


def over_low(total, group):
    total = total.reshape(group // 2, 2, total.shape[0] // group, LANES)
    return total[:, 0] + swap(total[:, 1], "dp", 1)


def pack(feed, last):
    lead = lax.reduce_precision(last, 8, 7)
    return jnp.concatenate([feed, lead, last - lead], axis=0).astype(BF16)


def unpack(message, feed_rows):
    message = message.astype(F32)
    rows = (message.shape[0] - feed_rows) // 2
    last = message[feed_rows : feed_rows + rows] + message[feed_rows + rows :]
    return message[:feed_rows], last


def over_high(feed, last, group):
    terms = [jnp.concatenate([feed[0], last[0]], axis=0)]
    for slot in range(1, group // 2):
        other = swap(pack(feed[slot], last[slot]), "dp", 2 * slot)
        terms.append(jnp.concatenate(unpack(other, feed.shape[1]), axis=0))
    total = tree_sum(terms)
    mask = group
    while mask < lax.axis_size("dp"):
        total = total + swap(total, "dp", mask)
        mask *= 2
    return total


def whole(shape):
    zeros = (0,) * len(shape)
    return pl.BlockSpec(shape, lambda i: zeros, pipeline_mode=pl.Buffered(1))


def each(shape):
    return pl.BlockSpec((1,) + tuple(shape[1:]), lambda i: (i,) + (0,) * (len(shape) - 1))


def struct(shape, dtype):
    return jax.ShapeDtypeStruct(shape, dtype)


def shards(
    tokens, modulation, cotangent,
    qkv_master, proj_master, up_master, down_master, bias_master,
    qkv_first, proj_first, up_first, down_first, bias_first,
    qkv_second, proj_second, up_second, down_second, bias_second,
):
    latents, span, width = tokens.shape
    hidden = up_master.shape[1]
    group = min(8, lax.axis_size("dp"))
    devices = lax.axis_size("dp") * lax.axis_size("shard")
    latent_total = latents * devices
    all_rows = latents * span

    bias_size = bias_master.shape[0]
    bias_block = jnp.pad(bias_master[None], ((0, 15), (0, 3 * width - bias_size)))
    first_w = jnp.concatenate([qkv_master, bias_block], axis=0).astype(BF16)
    first_high = swap(first_w, "shard", 2)
    first_low = swap(first_w, "shard", 1)
    first_ws = (first_w, first_low, first_high, swap(first_high, "shard", 1))
    rest_w = jnp.concatenate(
        [proj_master, down_master]
        + [up_master[:, i : i + width] for i in range(0, hidden, width)],
        axis=0,
    ).astype(BF16)
    rest_w, first_high = lax.optimization_barrier((rest_w, first_high))
    rest_high = swap(rest_w, "shard", 2)
    rest_low = swap(rest_w, "shard", 1)

    tok = (latents, span, width)
    mod = modulation.shape
    joint, attended, lse, moded, bias = pl.pallas_call(
        attend_kernel,
        grid=(latents,),
        in_specs=[each(tok), each(mod)] + [whole(w.shape) for w in first_ws],
        out_specs=[each((latents, span, 3 * width)), each(tok), each((latents, 8, span)), each(tok)]
        + [whole((4, bias_size))],
        out_shape=[
            struct((latents, span, 3 * width), BF16),
            struct(tok, BF16),
            struct((latents, 8, span), F32),
            struct(tok, BF16),
            struct((4, bias_size), F32),
        ],
        scratch_shapes=[pltpu.VMEM((width, 3 * width), BF16)],
        cost_estimate=pl.CostEstimate(flops=2 * 10**9, bytes_accessed=6 * 10**6, transcendentals=10**6),
        name="attend",
    )(tokens, modulation, *first_ws)
    rest_high, attended = lax.optimization_barrier((rest_high, attended))
    rest_ws = (rest_w, rest_low, rest_high, swap(rest_high, "shard", 1))

    feed_shape = (2, 2 * hidden * width // 4 // LANES, LANES)
    outs = pl.pallas_call(
        functools.partial(feed_kernel, group=group),
        grid=(latents,),
        in_specs=[each(tok), each(mod), each(tok), each(tok)]
        + [whole(w.shape) for w in rest_ws]
        + [whole(bias.shape)],
        out_specs=[each(tok), each(tok), each(tok), each((latents, 4, width))]
        + [whole((1, 2 * width + hidden)), whole((width, width))]
        + [whole(feed_shape)] * 2,
        out_shape=[
            struct(tok, BF16),
            struct(tok, F32),
            struct(tok, BF16),
            struct((latents, 4, width), F32),
            struct((1, 2 * width + hidden), F32),
            struct((width, width), F32),
        ]
        + [struct(feed_shape, F32)] * 2,
        scratch_shapes=[
            pltpu.VMEM((width, width), BF16),
            pltpu.VMEM((width, hidden), BF16),
            pltpu.VMEM((hidden, width), BF16),
            pltpu.VMEM((all_rows, hidden), BF16),
            pltpu.VMEM((all_rows, hidden), BF16),
            pltpu.VMEM((all_rows, width), BF16),
            pltpu.VMEM((all_rows, width), BF16),
            pltpu.VMEM((all_rows, width), BF16),
            pltpu.VMEM((all_rows, width), BF16),
            pltpu.VMEM((width, hidden), F32),
        ],
        cost_estimate=pl.CostEstimate(flops=8 * 10**9, bytes_accessed=16 * 10**6, transcendentals=2 * 10**6),
        name="feed",
    )(tokens, modulation, cotangent, attended, *rest_ws, bias)
    out_tokens, grad_middle, grad_attended, mod_feed, bias_feed, proj_term = outs[:6]
    feed_own, feed_far = over_core(outs[6], outs[7])

    last = 4 * width * (width // 4) // LANES
    last_chunk = -(-(last + 8) // (16 * group)) * 16
    last_shape = (2, last_chunk * group, LANES)
    split = latents // 2
    bias_sum = jnp.concatenate([jnp.zeros((1, 2 * width), F32), bias_feed], axis=1)
    full_shape = (width, 3 * width)

    def half(start, count, final, extra, aliases):
        def some(shape):
            return pl.BlockSpec(
                (1,) + tuple(shape[1:]), lambda i: (i + start,) + (0,) * (len(shape) - 1)
            )

        sums = [whole(bias_sum.shape), whole(full_shape)]
        ins = [some(a.shape) for a in (joint, attended, lse, grad_attended, moded)]
        scratch = [
            pltpu.VMEM((count * span, width), BF16),
            pltpu.VMEM((count * span, 3 * width), BF16),
        ]
        sums_scratch = [pltpu.VMEM(bias_sum.shape, F32), pltpu.VMEM(full_shape, F32)]
        sums_struct = [struct(bias_sum.shape, F32), struct(full_shape, F32)]
        return pl.pallas_call(
            functools.partial(attend_back_kernel, group=group, final=final),
            grid=(count,),
            in_specs=ins
            + ([whole(proj_term.shape)] + sums + [pl.BlockSpec(memory_space=pl.ANY)] if final else sums[:1]),
            out_specs=[some(joint.shape)] + ([whole(last_shape)] * 2 if final else sums),
            out_shape=[struct(joint.shape, BF16)]
            + ([struct(last_shape, F32)] * 2 if final else sums_struct),
            scratch_shapes=scratch + (sums_scratch if final else []),
            input_output_aliases=aliases,
            cost_estimate=pl.CostEstimate(flops=2 * 10**9, bytes_accessed=8 * 10**6, transcendentals=10**6),
            name="back_b" if final else "back_a",
        )(joint, attended, lse, grad_attended, moded, *extra)

    grad_joint, bias_sum, full = half(0, split, False, (bias_sum,), {})
    full, feed_far = lax.optimization_barrier((full, feed_far))
    feed_total = over_shard(feed_own, feed_far, BF16)
    grad_joint, keep, send = half(
        split, latents - split, True, (proj_term, bias_sum, full, grad_joint), {8: 0}
    )
    last_total = over_shard(*over_core(keep, send), F32)

    in_grad, mod_grad = pl.pallas_call(
        input_kernel,
        grid=(latents,),
        in_specs=[each(tok), each(mod), each(joint.shape), each(tok), each(mod_feed.shape)]
        + [whole(w.shape) for w in first_ws],
        out_specs=[each(tok), each(mod)],
        out_shape=[struct(tok, F32), struct(mod, F32)],
        scratch_shapes=[pltpu.VMEM((width, 3 * width), BF16)],
        cost_estimate=pl.CostEstimate(flops=2 * 10**9, bytes_accessed=8 * 10**6, transcendentals=0),
        name="input",
    )(tokens, modulation, grad_joint, grad_middle, mod_feed, *first_ws)

    feed_low = over_low(feed_total, group)
    last_low = over_low(last_total, group)
    feed_rows = feed_low.shape[1]
    total = over_high(feed_low, last_low, group) * (1.0 / latent_total)
    square = jnp.full((8, LANES), jnp.sum(total * total), F32)
    payload = pack(total[:feed_rows], jnp.concatenate([total[feed_rows:], square], axis=0))
    own = [payload] + [swap(payload, "dp", 2 * slot) for slot in range(1, group // 2)]
    square = tree_sum([unpack(p, feed_rows)[1][-8:] for p in own])
    own = jnp.stack(own)
    far = swap(own, "dp", 1)
    for axis, mask in (("shard", 1), ("shard", 2), ("dp", 1)):
        square = square + swap(square, axis, mask)
    factor = CLIP_NORM / jnp.maximum(jnp.sqrt(square[0:1, 0:1]), CLIP_NORM)

    states = (
        qkv_master, proj_master, up_master, down_master,
        qkv_first, proj_first, up_first, down_first,
        qkv_second, proj_second, up_second, down_second,
    )
    bias_rows = (bias_size // LANES, LANES)
    vmem = pl.BlockSpec(memory_space=pltpu.VMEM)
    shapes = [struct(s.shape, F32) for s in states]
    updated = pl.pallas_call(
        functools.partial(adam_kernel, group=group),
        in_specs=[pl.BlockSpec(memory_space=pltpu.SMEM)] + [vmem] * (2 + len(states)),
        out_specs=[vmem] * 17,
        out_shape=shapes[:4] + [struct(bias_rows, F32)] + shapes,
        scratch_shapes=[pltpu.VMEM(feed_shape[1:], F32), pltpu.VMEM(last_shape[1:], F32)],
        cost_estimate=pl.CostEstimate(flops=10**7, bytes_accessed=14 * 10**6, transcendentals=0),
        name="adam",
    )(factor, own, far, *states)
    bias_grad = updated[4].reshape(bias_size)
    bias_new = adam_step(bias_master, bias_grad, bias_first, bias_second, factor[0, 0])
    return (
        out_tokens, in_grad, mod_grad,
        *updated[:4], bias_grad,
        *updated[5:9], bias_new[0],
        *updated[9:13], bias_new[1],
        *updated[13:17], bias_new[2],
    )


def solution(mesh):
    data = P(("dp", "shard"), None, None)
    weight = P("shard", None)
    five = (weight, weight, weight, weight, P("shard"))
    return jax.shard_map(
        shards,
        mesh=mesh,
        in_specs=(data, data, data) + five * 3,
        out_specs=(data, data, data) + five * 4,
        check_vma=False,
    )
```

```python
import functools
import math

import jax
import jax.numpy as jnp
from jax import lax
from jax.experimental import pallas as pl
from jax.experimental.pallas import tpu as pltpu
from jax.sharding import PartitionSpec as P

HEADS = 6
STEP = 10

NORM_EPS = 1e-06
GELU_COEF = 0.7978845608028654
GELU_CUBIC = 0.044715
BETA_ONE = 0.9
BETA_TWO = 0.999
LEARN_RATE = 0.08
WEIGHT_DECAY = 0.01
ADAM_EPS = 1e-08
CLIP_NORM = 0.05

LANES = 128
BF16 = jnp.bfloat16
F32 = jnp.float32


def dot_nn(left, right):
    return lax.dot_general(left, right, (((1,), (0,)), ((), ())), preferred_element_type=F32)


def dot_nt(left, right):
    return lax.dot_general(left, right, (((1,), (1,)), ((), ())), preferred_element_type=F32)


def dot_tn(left, right):
    return lax.dot_general(left, right, (((0,), (0,)), ((), ())), preferred_element_type=F32)


def layer_norm(inputs):
    average = jnp.mean(inputs, axis=-1, keepdims=True)
    centered = inputs - average
    inv_std = lax.rsqrt(jnp.mean(centered * centered, axis=-1, keepdims=True) + NORM_EPS)
    return centered * inv_std, inv_std


def norm_back(normed, inv_std, upstream):
    return inv_std * (
        upstream
        - jnp.mean(upstream, axis=-1, keepdims=True)
        - normed * jnp.mean(upstream * normed, axis=-1, keepdims=True)
    )


def gelu_parts(inputs):
    square = inputs * inputs
    tangent = jnp.tanh(GELU_COEF * inputs * (1.0 + GELU_CUBIC * square))
    half = 0.5 * (1.0 + tangent)
    slopes = half + (0.5 * GELU_COEF) * inputs * (1.0 - tangent * tangent) * (
        1.0 + 3.0 * GELU_CUBIC * square
    )
    return inputs * half, slopes


def lane_half(shape, head):
    lanes = lax.broadcasted_iota(jnp.int32, shape, 1)
    return (lanes < LANES // 2) if head % 2 == 0 else (lanes >= LANES // 2)


def owners(refs):
    me = lax.axis_index("shard")
    return [(jnp.bitwise_xor(me, slot), ref) for slot, ref in enumerate(refs)]


def place(target, owner, rows, value):
    target[pl.ds(pl.multiple_of(owner * rows, 16), rows), :] = value


def attend_kernel(tokens, modulation, w0, w1, w2, w3, joint_out, attended_out, lse_out, moded_out, bias, weight):
    @pl.when(pl.program_id(0) == 0)
    def _():
        rows = weight.shape[0] // 4
        for owner, ref in owners((w0, w1, w2, w3)):
            place(weight, owner, rows, ref[:rows, :])
            bias[pl.ds(owner, 1), :] = ref[rows : rows + 1, : bias.shape[1]].astype(F32)

    width = tokens.shape[-1]
    normed, _ = layer_norm(tokens[0].astype(F32))
    mod = modulation[0]
    moded = (normed * (1.0 + mod[1:2]) + mod[0:1]).astype(BF16)
    moded_out[0] = moded
    joint = dot_nn(moded, weight[...])
    bias_full = bias[0:1, :]
    queries = (joint[:, :width] + bias_full[:, :width]).astype(BF16)
    key_rows = joint[:, width : 2 * width].astype(BF16)
    values = (joint[:, 2 * width :] + bias_full[:, width : 2 * width]).astype(BF16)
    joint_out[0, :, :width] = queries
    joint_out[0, :, width : 2 * width] = key_rows
    joint_out[0, :, 2 * width :] = values
    span = queries.shape[0]
    inverse = 1.0 / math.sqrt(width // HEADS)
    lanes = lax.broadcasted_iota(jnp.int32, (span, LANES), 1)
    columns = jnp.zeros((span, LANES), F32)
    for pair in range(HEADS // 2):
        part = slice(pair * LANES, (pair + 1) * LANES)
        halves = []
        for head in (0, 1):
            mask = lane_half((span, LANES), head)
            scaled = jnp.where(mask, queries[:, part].astype(F32) * inverse, 0.0).astype(BF16)
            scores = dot_nt(scaled, key_rows[:, part])
            top = jnp.max(scores, axis=-1, keepdims=True)
            exponent = jnp.exp(scores - top)
            total = jnp.sum(exponent, axis=-1, keepdims=True)
            probs = (exponent * (1.0 / total)).astype(BF16)
            halves.append(dot_nn(probs, values[:, part]))
            columns = jnp.where(lanes == 2 * pair + head, top + jnp.log(total), columns)
        attended_out[0, :, part] = jnp.where(
            lane_half((span, LANES), 0), halves[0], halves[1]
        ).astype(BF16)
    lse_out[0] = columns.T[:8]


def spread(get_rows, store, rows, start, count, chunk, group):
    me = jnp.bitwise_and(lax.axis_index("dp"), group - 1)
    unit = math.gcd(rows, chunk)
    for row in range(start, start + count, unit):
        slot = jnp.bitwise_xor(me, row // chunk)
        at = pl.multiple_of(slot * chunk + row % chunk, 8)
        store(pl.ds(at, unit), get_rows(row - start, unit))


def storer(keep, send, slot):
    target = (keep, send)[slot % 2]

    def store(rows, value):
        target[slot // 2, rows, :] = value

    return store


def feed_kernel(
    tokens, modulation, cotangent, attended,
    w0, w1, w2, w3, bias,
    out_tokens, grad_middle_out, grad_attended_out, mod_out, bias_out, proj_grad,
    keep, send,
    proj_w, up_w, down_w, act_all, pre_all, moded_all, branch_all, mixer_all, attended_all, up_full,
    *, group,
):
    step = pl.program_id(0)
    width = tokens.shape[-1]
    hidden = up_w.shape[1]

    @pl.when(step == 0)
    def _():
        rows, rows_down = width // 4, hidden // 4
        for owner, ref in owners((w0, w1, w2, w3)):
            place(proj_w, owner, rows, ref[:rows, :])
            place(down_w, owner, rows_down, ref[rows : rows + rows_down, :])
            for block in range(hidden // width):
                at = rows + rows_down + block * rows
                place(
                    up_w.at[:, block * width : (block + 1) * width], owner, rows, ref[at : at + rows, :]
                )
        bias_out[...] = jnp.zeros_like(bias_out)

    span = tokens.shape[1]
    here = pl.ds(pl.multiple_of(step * span, span), span)
    mod = modulation[0]
    bias_part = 2 * width
    bias_row = jnp.concatenate([bias[i : i + 1, :] for i in range(bias.shape[0])], axis=1)
    bias_proj = bias_row[:, bias_part : bias_part + width]
    bias_up = bias_row[:, 3 * width : 3 * width + hidden]
    bias_down = bias_row[:, 3 * width + hidden :]
    inputs = tokens[0].astype(F32)
    mixed = attended[0]
    attended_all[here, :] = mixed
    branch_mixer = dot_nn(mixed, proj_w[...]) + bias_proj
    middle = inputs + mod[2:3] * branch_mixer
    normed, inv_std = layer_norm(middle)
    moded = (normed * (1.0 + mod[4:5]) + mod[3:4]).astype(BF16)
    moded_all[here, :] = moded
    upstream = cotangent[0].astype(F32)
    grad_branch = upstream * mod[5:6]
    grad_branch_half = grad_branch.astype(BF16)
    branch_all[here, :] = grad_branch_half
    branch_feed = jnp.zeros((span, width), F32) + bias_down
    grad_moded = jnp.zeros((span, width), F32)
    block = width
    for start in range(0, hidden, block):
        cols = slice(start, start + block)
        act, slopes = gelu_parts(dot_nn(moded, up_w[:, cols]) + bias_up[:, cols])
        act = act.astype(BF16)
        act_all[here, cols] = act
        branch_feed = branch_feed + dot_nn(act, down_w[cols, :])
        grad_pre = dot_nt(grad_branch_half, down_w[cols, :]) * slopes
        bias_out[:, 3 * width + start : 3 * width + start + block] += jnp.sum(grad_pre, axis=0, keepdims=True)
        grad_pre = grad_pre.astype(BF16)
        pre_all[here, cols] = grad_pre
        grad_moded = grad_moded + dot_nt(grad_pre, up_w[:, cols])
    out_tokens[0] = (middle + mod[5:6] * branch_feed).astype(BF16)
    grad_middle = upstream + norm_back(normed, inv_std, grad_moded * (1.0 + mod[4:5]))
    grad_middle_out[0] = grad_middle
    grad_mixer = grad_middle * mod[2:3]
    grad_mixer_half = grad_mixer.astype(BF16)
    mixer_all[here, :] = grad_mixer_half
    grad_attended_out[0] = dot_nt(grad_mixer_half, proj_w[...]).astype(BF16)
    mod_out[0, 0:1] = jnp.sum(grad_middle * branch_mixer, axis=0, keepdims=True)
    mod_out[0, 1:2] = jnp.sum(grad_moded, axis=0, keepdims=True)
    mod_out[0, 2:3] = jnp.sum(grad_moded * normed, axis=0, keepdims=True)
    mod_out[0, 3:4] = jnp.sum(upstream * branch_feed, axis=0, keepdims=True)
    bias_out[:, 2 * width : 3 * width] += jnp.sum(grad_mixer, axis=0, keepdims=True)
    bias_out[:, 3 * width + hidden :] += jnp.sum(grad_branch, axis=0, keepdims=True)

    @pl.when(step == pl.num_programs(0) - 1)
    def _():
        me = lax.axis_index("shard")
        rows = hidden // 4
        rows_up = width // 4
        chunk = keep.shape[1] // group
        half = keep.shape[1] // 2
        for slot in (1, 3, 0, 2):
            owner = jnp.bitwise_xor(me, slot)
            mine = act_all[:, pl.ds(pl.multiple_of(owner * rows, LANES), rows)]
            term = dot_tn(mine, branch_all[...])

            def down_rows(start, unit, term=term):
                col, row = start // rows, start % rows
                return term[row : row + unit, col * LANES : (col + 1) * LANES]

            spread(down_rows, storer(keep, send, slot), rows, 0, half, chunk, group)
        up_full[...] = dot_tn(moded_all[...], pre_all[...])
        for slot in range(4):
            owner = jnp.bitwise_xor(me, slot)

            def up_rows(start, unit, owner=owner):
                col, row = start // rows_up, start % rows_up
                at = pl.multiple_of(owner * rows_up + row, 8)
                return up_full[pl.ds(at, unit), col * LANES : (col + 1) * LANES]

            spread(up_rows, storer(keep, send, slot), rows_up, half, half, chunk, group)
        proj_grad[...] = dot_tn(attended_all[...], mixer_all[...])


def attend_back_kernel(joint, attended, lse, grad_attended, moded, *rest, group, final):
    if final:
        proj_grad, bias_before, full_before, _, grad_joint_out, keep, send = rest[:7]
        moded_all, joint_all, bias_sum, full = rest[7:]
    else:
        bias_before, grad_joint_out, bias_sum, full = rest[:4]
        moded_all, joint_all = rest[4:]
    step = pl.program_id(0)
    width = attended.shape[-1]
    span = attended.shape[1]
    here = pl.ds(pl.multiple_of(step * span, span), span)

    @pl.when(step == 0)
    def _():
        bias_sum[...] = bias_before[...]

    moded_all[here, :] = moded[0]
    inverse = 1.0 / math.sqrt(width // HEADS)
    lanes = lax.broadcasted_iota(jnp.int32, (span, LANES), 1)
    deltas = jnp.zeros((span, LANES), F32)
    for pair in range(HEADS // 2):
        part = slice(pair * LANES, (pair + 1) * LANES)
        products = grad_attended[0, :, part].astype(F32) * attended[0, :, part].astype(F32)
        for head in (0, 1):
            mask = lane_half((span, LANES), head)
            column = jnp.sum(jnp.where(mask, products, 0.0), axis=-1, keepdims=True)
            deltas = jnp.where(lanes == 2 * pair + head, column, deltas)
    delta_rows = deltas.T[:8]
    for pair in range(HEADS // 2):
        part = slice(pair * LANES, (pair + 1) * LANES)
        queries = joint[0, :, pair * LANES : (pair + 1) * LANES]
        keys = joint[0, :, width + pair * LANES : width + (pair + 1) * LANES]
        values = joint[0, :, 2 * width + pair * LANES : 2 * width + (pair + 1) * LANES]
        upstream = grad_attended[0, :, part]
        results = []
        for head in (0, 1):
            index = 2 * pair + head
            mask = lane_half((span, LANES), head)
            masked_keys = jnp.where(mask, keys.astype(F32) * inverse, 0.0).astype(BF16)
            masked_values = jnp.where(mask, values.astype(F32), 0.0).astype(BF16)
            probs = jnp.exp(dot_nt(masked_keys, queries) - lse[0, index : index + 1, :])
            grad_values = dot_nn(probs.astype(BF16), upstream)
            grad_probs = dot_nt(masked_values, upstream)
            grad_scores = (probs * (grad_probs - delta_rows[index : index + 1, :]) * inverse).astype(BF16)
            grad_keys = dot_nn(grad_scores, queries)
            grad_queries = dot_tn(grad_scores, keys)
            results.append((grad_queries, grad_keys, grad_values))
        mask = lane_half((span, LANES), 0)
        for at, (low, high) in enumerate(zip(*results)):
            value = jnp.where(mask, low, high)
            cols = slice(at * width + pair * LANES, at * width + (pair + 1) * LANES)
            half = value.astype(BF16)
            grad_joint_out[0, :, cols] = half
            joint_all[here, cols] = half
            if at != 1:
                place = (at // 2) * width + pair * LANES
                bias_sum[:, place : place + LANES] += jnp.sum(value, axis=0, keepdims=True)

    @pl.when(step == pl.num_programs(0) - 1)
    def _():
        full[...] = dot_tn(moded_all[...], joint_all[...])
        if not final:
            return
        full[...] += full_before[...]
        me = lax.axis_index("shard")
        rows = width // 4
        cols_joint = 3 * width // LANES
        tail = 4 * width // LANES * rows
        total = keep.shape[1]
        chunk = total // group
        bias_rows = bias_sum.shape[1] // 4 // LANES
        for slot in range(4):
            owner = jnp.bitwise_xor(me, slot)
            unit_tail = math.gcd(rows, chunk)
            bias_at = owner * bias_rows * LANES
            block = jnp.concatenate(
                [
                    bias_sum[:, pl.ds(pl.multiple_of(bias_at + i * LANES, LANES), LANES)]
                    for i in range(bias_rows)
                ]
                + [jnp.zeros((unit_tail - bias_rows, LANES), F32)],
                axis=0,
            )

            def part_rows(start, unit, owner=owner, block=block):
                if start == tail:
                    return block
                if start > tail:
                    return jnp.zeros((unit, LANES), F32)
                col, row = start // rows, start % rows
                at = pl.multiple_of(owner * rows + row, 8)
                if col < cols_joint:
                    return full[pl.ds(at, unit), col * LANES : (col + 1) * LANES]
                col -= cols_joint
                return proj_grad[pl.ds(at, unit), col * LANES : (col + 1) * LANES]

            spread(part_rows, storer(keep, send, slot), rows, 0, total, chunk, group)


def input_kernel(tokens, modulation, grad_joint, grad_middle, mod_feed, w0, w1, w2, w3, in_grad, mod_grad, weight):
    @pl.when(pl.program_id(0) == 0)
    def _():
        rows = weight.shape[0] // 4
        for owner, ref in owners((w0, w1, w2, w3)):
            place(weight, owner, rows, ref[:rows, :])

    mod = modulation[0]
    normed, inv_std = layer_norm(tokens[0].astype(F32))
    grad_moded = dot_nt(grad_joint[0], weight[...])
    in_grad[0] = grad_middle[0] + norm_back(normed, inv_std, grad_moded * (1.0 + mod[1:2]))
    mod_grad[0, 0:1] = jnp.sum(grad_moded, axis=0, keepdims=True)
    mod_grad[0, 1:2] = jnp.sum(grad_moded * normed, axis=0, keepdims=True)
    mod_grad[0, 2:6] = mod_feed[0]


def adam_kernel(
    factor_ref, own, far,
    qkv_w, proj_w, up_w, down_w,
    qkv_m, proj_m, up_m, down_m,
    qkv_v, proj_v, up_v, down_v,
    qkv_g, proj_g, up_g, down_g, bias_g,
    qkv_nw, proj_nw, up_nw, down_nw,
    qkv_nm, proj_nm, up_nm, down_nm,
    qkv_nv, proj_nv, up_nv, down_nv,
    feed_all, part_all,
    *, group,
):
    me = jnp.bitwise_and(lax.axis_index("dp"), group - 1)
    factor = factor_ref[0, 0]
    base = 0
    for target in (feed_all, part_all):
        chunk = target.shape[0] // group
        for slot in range(group):
            source = own if slot % 2 == 0 else far
            at = jnp.bitwise_xor(me, slot) * chunk
            value = source[slot // 2, base : base + chunk, :].astype(F32)
            if base:
                rest = (source.shape[1] - base) // 2
                value = value + source[slot // 2, base + rest : base + rest + chunk, :].astype(F32)
            target[pl.ds(pl.multiple_of(at, 8), chunk), :] = value
        base += chunk

    base = 0
    for source, start, refs in (
        (feed_all, True, (down_w, down_m, down_v, down_g, down_nw, down_nm, down_nv)),
        (feed_all, False, (up_w, up_m, up_v, up_g, up_nw, up_nm, up_nv)),
        (part_all, True, (qkv_w, qkv_m, qkv_v, qkv_g, qkv_nw, qkv_nm, qkv_nv)),
        (part_all, False, (proj_w, proj_m, proj_v, proj_g, proj_nw, proj_nm, proj_nv)),
    ):
        base = 0 if start else base
        w, m, v, g_out, w_out, m_out, v_out = refs
        rows, cols = w.shape
        for col in range(cols // LANES):
            at = slice(col * LANES, (col + 1) * LANES)
            grad = source[base : base + rows, :]
            g_out[:, at] = grad
            w_out[:, at], m_out[:, at], v_out[:, at] = adam_step(w[:, at], grad, m[:, at], v[:, at], factor)
            base += rows
    bias_g[...] = part_all[base : base + bias_g.shape[0], :]


def adam_step(master, grad, first, second, factor):
    clipped = grad * factor
    first = BETA_ONE * first + (1.0 - BETA_ONE) * clipped
    second = BETA_TWO * second + (1.0 - BETA_TWO) * clipped * clipped
    first_hat = first * (1.0 / (1.0 - BETA_ONE**STEP))
    second_hat = second * (1.0 / (1.0 - BETA_TWO**STEP))
    master = master - LEARN_RATE * (
        first_hat / (jnp.sqrt(second_hat) + ADAM_EPS) + WEIGHT_DECAY * master
    )
    return master, first, second


def swap(value, axis, mask):
    size = lax.axis_size(axis)
    return lax.ppermute(value, axis, [(i, i ^ mask) for i in range(size)])


def tree_sum(parts):
    while len(parts) > 1:
        parts = [parts[i] + parts[i + 1] for i in range(0, len(parts), 2)]
    return parts[0]


def over_core(keep, send):
    other = swap(send, "shard", 1)
    return keep[0] + other[0], keep[1] + other[1]


def over_shard(own, far, wire):
    return own + swap(far.astype(wire), "shard", 2).astype(F32)


def over_low(total, group):
    total = total.reshape(group // 2, 2, total.shape[0] // group, LANES)
    return total[:, 0] + swap(total[:, 1], "dp", 1)


def pack(feed, last):
    lead = lax.reduce_precision(last, 8, 7)
    return jnp.concatenate([feed, lead, last - lead], axis=0).astype(BF16)


def unpack(message, feed_rows):
    message = message.astype(F32)
    rows = (message.shape[0] - feed_rows) // 2
    last = message[feed_rows : feed_rows + rows] + message[feed_rows + rows :]
    return message[:feed_rows], last


def over_high(feed, last, group):
    terms = [jnp.concatenate([feed[0], last[0]], axis=0)]
    for slot in range(1, group // 2):
        other = swap(pack(feed[slot], last[slot]), "dp", 2 * slot)
        terms.append(jnp.concatenate(unpack(other, feed.shape[1]), axis=0))
    total = tree_sum(terms)
    mask = group
    while mask < lax.axis_size("dp"):
        total = total + swap(total, "dp", mask)
        mask *= 2
    return total


def whole(shape):
    zeros = (0,) * len(shape)
    return pl.BlockSpec(shape, lambda i: zeros, pipeline_mode=pl.Buffered(1))


def each(shape):
    return pl.BlockSpec((1,) + tuple(shape[1:]), lambda i: (i,) + (0,) * (len(shape) - 1))


def struct(shape, dtype):
    return jax.ShapeDtypeStruct(shape, dtype)


def shards(
    tokens, modulation, cotangent,
    qkv_master, proj_master, up_master, down_master, bias_master,
    qkv_first, proj_first, up_first, down_first, bias_first,
    qkv_second, proj_second, up_second, down_second, bias_second,
):
    latents, span, width = tokens.shape
    hidden = up_master.shape[1]
    group = min(8, lax.axis_size("dp"))
    devices = lax.axis_size("dp") * lax.axis_size("shard")
    latent_total = latents * devices
    all_rows = latents * span

    bias_size = bias_master.shape[0]
    bias_block = jnp.pad(bias_master[None], ((0, 15), (0, 3 * width - bias_size)))
    first_w = jnp.concatenate([qkv_master, bias_block], axis=0).astype(BF16)
    first_high = swap(first_w, "shard", 2)
    first_low = swap(first_w, "shard", 1)
    first_ws = (first_w, first_low, first_high, swap(first_high, "shard", 1))
    rest_w = jnp.concatenate(
        [proj_master, down_master]
        + [up_master[:, i : i + width] for i in range(0, hidden, width)],
        axis=0,
    ).astype(BF16)
    rest_w, first_high = lax.optimization_barrier((rest_w, first_high))
    rest_high = swap(rest_w, "shard", 2)
    rest_low = swap(rest_w, "shard", 1)

    tok = (latents, span, width)
    mod = modulation.shape
    joint, attended, lse, moded, bias = pl.pallas_call(
        attend_kernel,
        grid=(latents,),
        in_specs=[each(tok), each(mod)] + [whole(w.shape) for w in first_ws],
        out_specs=[each((latents, span, 3 * width)), each(tok), each((latents, 8, span)), each(tok)]
        + [whole((4, bias_size))],
        out_shape=[
            struct((latents, span, 3 * width), BF16),
            struct(tok, BF16),
            struct((latents, 8, span), F32),
            struct(tok, BF16),
            struct((4, bias_size), F32),
        ],
        scratch_shapes=[pltpu.VMEM((width, 3 * width), BF16)],
        cost_estimate=pl.CostEstimate(flops=2 * 10**9, bytes_accessed=6 * 10**6, transcendentals=10**6),
        name="attend",
    )(tokens, modulation, *first_ws)
    rest_high, attended = lax.optimization_barrier((rest_high, attended))
    rest_ws = (rest_w, rest_low, rest_high, swap(rest_high, "shard", 1))

    feed_shape = (2, 2 * hidden * width // 4 // LANES, LANES)
    outs = pl.pallas_call(
        functools.partial(feed_kernel, group=group),
        grid=(latents,),
        in_specs=[each(tok), each(mod), each(tok), each(tok)]
        + [whole(w.shape) for w in rest_ws]
        + [whole(bias.shape)],
        out_specs=[each(tok), each(tok), each(tok), each((latents, 4, width))]
        + [whole((1, 4 * width + hidden)), whole((width, width))]
        + [whole(feed_shape)] * 2,
        out_shape=[
            struct(tok, BF16),
            struct(tok, F32),
            struct(tok, BF16),
            struct((latents, 4, width), F32),
            struct((1, 4 * width + hidden), F32),
            struct((width, width), F32),
        ]
        + [struct(feed_shape, F32)] * 2,
        scratch_shapes=[
            pltpu.VMEM((width, width), BF16),
            pltpu.VMEM((width, hidden), BF16),
            pltpu.VMEM((hidden, width), BF16),
            pltpu.VMEM((all_rows, hidden), BF16),
            pltpu.VMEM((all_rows, hidden), BF16),
            pltpu.VMEM((all_rows, width), BF16),
            pltpu.VMEM((all_rows, width), BF16),
            pltpu.VMEM((all_rows, width), BF16),
            pltpu.VMEM((all_rows, width), BF16),
            pltpu.VMEM((width, hidden), F32),
        ],
        cost_estimate=pl.CostEstimate(flops=8 * 10**9, bytes_accessed=16 * 10**6, transcendentals=2 * 10**6),
        name="feed",
    )(tokens, modulation, cotangent, attended, *rest_ws, bias)
    out_tokens, grad_middle, grad_attended, mod_feed, bias_feed, proj_term = outs[:6]
    feed_own, feed_far = over_core(outs[6], outs[7])

    last = 4 * width * (width // 4) // LANES
    last_chunk = -(-(last + 8) // (16 * group)) * 16
    last_shape = (2, last_chunk * group, LANES)
    split = latents // 2
    bias_sum = bias_feed
    full_shape = (width, 3 * width)

    def half(start, count, final, extra, aliases):
        def some(shape):
            return pl.BlockSpec(
                (1,) + tuple(shape[1:]), lambda i: (i + start,) + (0,) * (len(shape) - 1)
            )

        sums = [whole(bias_sum.shape), whole(full_shape)]
        ins = [some(a.shape) for a in (joint, attended, lse, grad_attended, moded)]
        scratch = [
            pltpu.VMEM((count * span, width), BF16),
            pltpu.VMEM((count * span, 3 * width), BF16),
        ]
        sums_scratch = [pltpu.VMEM(bias_sum.shape, F32), pltpu.VMEM(full_shape, F32)]
        sums_struct = [struct(bias_sum.shape, F32), struct(full_shape, F32)]
        return pl.pallas_call(
            functools.partial(attend_back_kernel, group=group, final=final),
            grid=(count,),
            in_specs=ins
            + ([whole(proj_term.shape)] + sums + [pl.BlockSpec(memory_space=pl.ANY)] if final else sums[:1]),
            out_specs=[some(joint.shape)] + ([whole(last_shape)] * 2 if final else sums),
            out_shape=[struct(joint.shape, BF16)]
            + ([struct(last_shape, F32)] * 2 if final else sums_struct),
            scratch_shapes=scratch + (sums_scratch if final else []),
            input_output_aliases=aliases,
            cost_estimate=pl.CostEstimate(flops=2 * 10**9, bytes_accessed=8 * 10**6, transcendentals=10**6),
            name="back_b" if final else "back_a",
        )(joint, attended, lse, grad_attended, moded, *extra)

    grad_joint, bias_sum, full = half(0, split, False, (bias_sum,), {})
    full, feed_far = lax.optimization_barrier((full, feed_far))
    feed_total = over_shard(feed_own, feed_far, BF16)
    grad_joint, keep, send = half(
        split, latents - split, True, (proj_term, bias_sum, full, grad_joint), {8: 0}
    )
    last_total = over_shard(*over_core(keep, send), F32)

    in_grad, mod_grad = pl.pallas_call(
        input_kernel,
        grid=(latents,),
        in_specs=[each(tok), each(mod), each(joint.shape), each(tok), each(mod_feed.shape)]
        + [whole(w.shape) for w in first_ws],
        out_specs=[each(tok), each(mod)],
        out_shape=[struct(tok, F32), struct(mod, F32)],
        scratch_shapes=[pltpu.VMEM((width, 3 * width), BF16)],
        cost_estimate=pl.CostEstimate(flops=2 * 10**9, bytes_accessed=8 * 10**6, transcendentals=0),
        name="input",
    )(tokens, modulation, grad_joint, grad_middle, mod_feed, *first_ws)

    feed_low = over_low(feed_total, group)
    last_low = over_low(last_total, group)
    feed_rows = feed_low.shape[1]
    total = over_high(feed_low, last_low, group) * (1.0 / latent_total)
    square = jnp.full((8, LANES), jnp.sum(total * total), F32)
    payload = pack(total[:feed_rows], jnp.concatenate([total[feed_rows:], square], axis=0))
    own = [payload] + [swap(payload, "dp", 2 * slot) for slot in range(1, group // 2)]
    square = tree_sum([unpack(p, feed_rows)[1][-8:] for p in own])
    own = jnp.stack(own)
    far = swap(own, "dp", 1)
    for axis, mask in (("shard", 1), ("shard", 2), ("dp", 1)):
        square = square + swap(square, axis, mask)
    factor = CLIP_NORM / jnp.maximum(jnp.sqrt(square[0:1, 0:1]), CLIP_NORM)

    states = (
        qkv_master, proj_master, up_master, down_master,
        qkv_first, proj_first, up_first, down_first,
        qkv_second, proj_second, up_second, down_second,
    )
    bias_rows = (bias_size // LANES, LANES)
    vmem = pl.BlockSpec(memory_space=pltpu.VMEM)
    shapes = [struct(s.shape, F32) for s in states]
    updated = pl.pallas_call(
        functools.partial(adam_kernel, group=group),
        in_specs=[pl.BlockSpec(memory_space=pltpu.SMEM)] + [vmem] * (2 + len(states)),
        out_specs=[vmem] * 17,
        out_shape=shapes[:4] + [struct(bias_rows, F32)] + shapes,
        scratch_shapes=[pltpu.VMEM(feed_shape[1:], F32), pltpu.VMEM(last_shape[1:], F32)],
        cost_estimate=pl.CostEstimate(flops=10**7, bytes_accessed=14 * 10**6, transcendentals=0),
        name="adam",
    )(factor, own, far, *states)
    bias_grad = updated[4].reshape(bias_size)
    bias_new = adam_step(bias_master, bias_grad, bias_first, bias_second, factor[0, 0])
    return (
        out_tokens, in_grad, mod_grad,
        *updated[:4], bias_grad,
        *updated[5:9], bias_new[0],
        *updated[9:13], bias_new[1],
        *updated[13:17], bias_new[2],
    )


def solution(mesh):
    data = P(("dp", "shard"), None, None)
    weight = P("shard", None)
    five = (weight, weight, weight, weight, P("shard"))
    return jax.shard_map(
        shards,
        mesh=mesh,
        in_specs=(data, data, data) + five * 3,
        out_specs=(data, data, data) + five * 4,
        check_vma=False,
    )
```
